32 devices in a mesh: rows: 8 (over z, y), grp: 4 (over x, core).
Axes of the slice: x: 2, y: 2, z: 4, core: 2. Of those that a mesh axis runs over, the one named last changes fastest.
Arguments:
- a_vals: bfloat16 [2048, 16384], P(('rows', 'grp')), may hold values from -0.75 to 0.75
- a_cols: int32 [2048, 4], P(('rows', 'grp')), may hold values from 0 to 2047, as said below
- p_vals: bfloat16 [2048, 16384], P(('rows', 'grp')), may hold values from -0.25 to 0.25
- new_rows: int32 [2048], P(('rows', 'grp')), may hold values from 0 to 7, as said below
Outputs:
- a_moved: bfloat16 [2048, 16384], P(('rows', 'grp'))
- coarse: bfloat16 [2048, 768], P(('rows', 'grp'))
The draws below stay inside these ranges and needn't reach their ends.
Inputs may be any that keep to these rules, and one draw needn't show every extreme that they name: `a_cols`: the first entry of row i is i itself; every entry names a block row whose slab is slab(i) - 1, slab(i) or slab(i) + 1, with any grp index. `new_rows`: the rows of one device go to each rows index either none or exactly 16 at a time, and for each grp index every rows index receives exactly 64 rows.
All inputs are finite; a program needn't handle non-finite values.
Results may differ from the reference program's by a relative error of at most 0.005.
Values may be sent and summed in bfloat16 or wider, within the bound.
No kernel may reach another device: no remote copies, remote signals or barrier semaphores. Data moves between devices by JAX's collectives and lax.ppermute only.
A program may use at most 192 MiB of HBM per device.

```python
import jax
import jax.numpy as jnp
from jax import lax

B = 64
KA = 4
RB = 64
CBR = 4
NB = 2048
CAP = 16
N_ROWS = 8
N_GRP = 4


def draw_a_cols(key, part):
    first_key, second_key, third_key = jax.random.split(jax.random.fold_in(key, 11), 3)
    positions = jnp.arange(NB, dtype=jnp.int32)
    device_of = positions // RB
    slab_of = device_of // N_GRP
    shifts = jax.random.randint(first_key, (NB, KA), -1, 2)
    slab_col = slab_of[:, None] + shifts
    slab_col = jnp.where((slab_col < 0) | (slab_col >= N_ROWS), slab_of[:, None], slab_col)
    grp_col = jax.random.randint(third_key, (NB, KA), 0, N_GRP)
    offsets = jax.random.randint(second_key, (NB, KA), 0, RB)
    columns = (slab_col * N_GRP + grp_col) * RB + offsets
    columns = columns.at[:, 0].set(positions)
    return columns.astype(jnp.int32)


def draw_new_rows(key, part):
    first_key, second_key = jax.random.split(jax.random.fold_in(key, 23))
    devices_all = N_ROWS * N_GRP
    shuffle = jax.random.permutation(first_key, N_ROWS)
    parity_keys = (shuffle[None, :] - jnp.arange(2)[:, None]) % 2 * N_ROWS + jnp.arange(N_ROWS)[None, :]
    dest_lists = jnp.argsort(parity_keys, axis=1)[:, :N_ROWS // 2]
    scores = jax.random.randint(second_key, (devices_all, RB), 0, 1 << 20) * RB + jnp.arange(RB)[None, :]
    ordering = jnp.argsort(scores, axis=1)
    ranking = jnp.argsort(ordering, axis=1)
    slab_of = jnp.arange(devices_all) // N_GRP
    dest = dest_lists[(slab_of % 2)[:, None], ranking // CAP]
    return dest.reshape(NB).astype(jnp.int32)


def block_scale(key, extent, cuts, least, largest):
    def one(dim, blocks):
        heights = jax.random.uniform(jax.random.fold_in(jax.random.fold_in(key, 6), dim), (blocks,), jnp.float32, least / len(cuts), largest / len(cuts))
        return jnp.repeat(jnp.exp(heights), extent[dim] // blocks).reshape((-1,) + (1,) * (len(extent) - dim - 1))

    loudness = one(*cuts[0])
    for cut in cuts[1:]:
        loudness = loudness * one(*cut)
    return loudness


def gaussian(rng, extent, scale, bound, cuts=(), kind=jnp.bfloat16):
    values = jax.random.normal(rng, extent, jnp.float32) * scale
    if len(cuts) > 0:
        values = block_scale(rng, extent, cuts, -0.22, 0.18) * values
    return jnp.clip(values, min=-bound, max=bound).astype(kind)


def setup_inputs(seed: int = 0) -> dict:
    streams_of = jax.random.split(jax.random.key(seed), 5)
    a_vals = gaussian(streams_of[0], (NB, B * KA * B), B ** -0.5, 0.75, ((0, 32),))
    a_cols = draw_a_cols(jax.random.fold_in(streams_of[4], 71), 0)
    p_vals = gaussian(streams_of[2], (NB, B * CBR * B), (8 * B) ** -0.5, 0.25, ((0, 32),))
    new_rows = draw_new_rows(jax.random.fold_in(streams_of[4], 71), 0)
    return dict(a_vals=a_vals, a_cols=a_cols, p_vals=p_vals, new_rows=new_rows)


def reference(a_vals, a_cols, p_vals, new_rows):
    devices_all = N_ROWS * N_GRP
    blocks_dev = a_vals.reshape(devices_all, RB, B, KA, B)
    cols_dev = a_cols.reshape(devices_all, RB, KA)

    def per_device(item):
        blocks, cols, start = item
        slab_here = start // N_GRP
        gathered = p_vals[cols].reshape(RB, KA, B, CBR * B).astype(jnp.float32)
        window_slot = (cols // RB) // N_GRP - slab_here + 1
        pieces = []
        for offset in range(3):
            kept_mask = (window_slot == offset).astype(jnp.float32)
            masked = blocks.astype(jnp.float32) * kept_mask[:, None, :, None]
            pieces.append(jnp.einsum("jake,jkef->jaf", masked, gathered))
        products = jnp.stack(pieces, axis=2).reshape(RB * B, 3 * CBR * B).astype(jnp.bfloat16)
        own_rows = lax.dynamic_slice_in_dim(p_vals, (start * RB).astype(jnp.int32), RB, 0)
        own_rows = own_rows.reshape(RB * B, CBR * B)
        return lax.dot_general(own_rows, products, (((0,), (0,)), ((), ())), preferred_element_type=jnp.float32)

    partials = lax.map(per_device, (blocks_dev, cols_dev, jnp.arange(devices_all, dtype=jnp.int32)))
    partials = partials.reshape(N_ROWS, N_GRP, CBR * B, 3 * CBR * B)
    coarse = jnp.sum(partials, axis=1).reshape(N_ROWS * CBR * B, 3 * CBR * B).astype(jnp.bfloat16)
    positions = jnp.arange(NB, dtype=jnp.int32)
    grp_index = (positions // RB) % N_GRP
    target = new_rows * N_GRP + grp_index
    ordering = jnp.argsort(target, stable=True)
    a_moved = a_vals[ordering]
    return (a_moved, coarse)
```

```python
import functools

import jax
import jax.numpy as jnp
from jax import lax
from jax.experimental import pallas as pl
from jax.experimental.pallas import tpu as pltpu
from jax.sharding import PartitionSpec as P

B = 64
UNROLL = 8


def xor_permute(value, axis, bit):
    count = lax.axis_size(axis)
    return lax.ppermute(value, axis, [(i, i ^ bit) for i in range(count)])


def scatter_kernel(parts, band, row_count, where_ref, *refs):
    cols = refs[:parts]
    a_refs = refs[parts : 2 * parts]
    p_refs = refs[2 * parts : 3 * parts]
    outs = refs[3 * parts : 3 * parts + 3]
    sums, order = refs[3 * parts + 3 :]
    rows_pos, grp_pos = where_ref[0], where_ref[1]
    groups = where_ref[2]
    slab_rows = row_count * groups
    odd = lax.rem(rows_pos, 2)
    entries = row_count * band
    dummy = 3 * row_count

    def clear(step, _):
        sums[pl.ds(pl.multiple_of(step * B, B), B), :] = jnp.zeros((B, sums.shape[1]), sums.dtype)
        return 0

    lax.fori_loop(0, dummy + 1, clear, 0)

    for part in range(parts):
        col_ref, a_ref, p_ref = cols[part], a_refs[part], p_refs[part]

        def collect(step, found):
            col = col_ref[step]
            device = lax.div(col, row_count)
            owner = lax.rem(device, groups)
            slab = lax.div(device, groups)
            near = slab - rows_pos
            side = jnp.where(odd == 1, -near, near)
            slot = jnp.where(near == 0, 0, jnp.where(side == 1, 1, 2))
            target = slot * row_count + lax.rem(col, row_count)
            order[found] = step * (4 * row_count) + target
            return found + jnp.where(owner == grp_pos, 1, 0)

        count = lax.fori_loop(0, entries, collect, 0, unroll=8)
        for pad in range(UNROLL):
            order[count + pad] = dummy

        def batch(step, _):
            terms = []
            for lane in range(UNROLL):
                code = order[step * UNROLL + lane]
                entry = lax.div(code, 4 * row_count)
                target = lax.rem(code, 4 * row_count)
                row = lax.div(entry, band)
                k = lax.rem(entry, band)
                start = pl.multiple_of(row * B, B)
                half = pl.multiple_of(lax.div(k, 2) * (2 * B), 2 * B)
                block = a_ref[pl.ds(start, B), pl.ds(half, 2 * B)]
                left = p_ref[pl.ds(start, B), :]
                term = lax.dot_general(
                    block, left, (((0,), (0,)), ((), ())), preferred_element_type=jnp.float32
                )
                terms.append((jnp.where(lax.rem(k, 2) == 1, term[B:], term[:B]), target))
            for term, target in terms:
                at = pl.ds(pl.multiple_of(target * B, B), B)
                sums[at, :] = sums[at, :] + term
            return 0

        lax.fori_loop(0, lax.div(count + UNROLL - 1, UNROLL), batch, 0)

    for slot in range(3):
        def emit(step, _):
            at = pl.multiple_of(step * B, B)
            outs[slot][pl.ds(at, B), :] = sums[pl.ds(slot * row_count * B + at, B), :].astype(
                outs[slot].dtype
            )
            return 0

        lax.fori_loop(0, row_count, emit, 0)


def scatter_products(where, cols, a_parts, p_parts, band, row_count):
    parts = len(cols)
    width = p_parts[0].shape[1]
    smem = pl.BlockSpec(memory_space=pltpu.SMEM)
    vmem = pl.BlockSpec(memory_space=pltpu.VMEM)
    shape = jax.ShapeDtypeStruct((row_count * B, width), jnp.bfloat16)
    return pl.pallas_call(
        functools.partial(scatter_kernel, parts, band, row_count),
        out_shape=(shape,) * 3,
        in_specs=[smem] * (1 + parts) + [vmem] * (2 * parts),
        out_specs=(vmem,) * 3,
        scratch_shapes=[
            pltpu.VMEM(((3 * row_count + 1) * B, width), jnp.float32),
            pltpu.SMEM((row_count * band + UNROLL,), jnp.int32),
        ],
        compiler_params=pltpu.CompilerParams(vmem_limit_bytes=48 << 20),
        cost_estimate=pl.CostEstimate(
            flops=parts * row_count * 2 * B * B * width * 2,
            bytes_accessed=parts * 8 * row_count * B * width,
            transcendentals=0,
        ),
    )(where, *[c.reshape(-1) for c in cols], *a_parts, *p_parts)


def contract(left, right):
    return lax.dot_general(
        left, right, (((0,), (0,)), ((), ())), preferred_element_type=jnp.float32
    )


def select_rows(picker, source):
    return jnp.dot(picker, source, preferred_element_type=jnp.float32).astype(jnp.bfloat16)


def migrate(a_vals, new_rows):
    row_count, row_width = a_vals.shape
    rows_total = lax.axis_size("rows")
    capacity = max(2, 2 * row_count // rows_total)
    slot_total = rows_total * capacity
    dest_hot = (new_rows[:, None] == jnp.arange(rows_total, dtype=jnp.int32)[None, :]).astype(
        jnp.int32
    )
    ranking = jnp.sum((jnp.cumsum(dest_hot, axis=0) - 1) * dest_hot, axis=1)
    slot_of = new_rows * capacity + ranking
    slot_ids = jnp.arange(slot_total, dtype=jnp.int32)
    sender = (slot_ids[:, None] == slot_of[None, :]).astype(jnp.bfloat16)
    outgoing = select_rows(sender, a_vals)
    filled = jnp.sum(sender, axis=1)
    incoming, flags = (
        lax.all_to_all(
            outgoing.reshape(rows_total, capacity, row_width),
            "rows",
            split_axis=0,
            concat_axis=0,
            tiled=True,
        ),
        lax.all_to_all(
            filled.reshape(rows_total, capacity), "rows", split_axis=0, concat_axis=0, tiled=True
        ),
    )
    flat_flags = flags.reshape(slot_total).astype(jnp.float32)
    position = jnp.cumsum(flat_flags) - 1.0
    flat_rows = incoming.reshape(slot_total, row_width)
    wanted = jnp.arange(row_count, dtype=jnp.float32)
    receiver = ((position[None, :] == wanted[:, None]) & (flat_flags[None, :] > 0.0)).astype(
        jnp.bfloat16
    )
    return select_rows(receiver, flat_rows)


def galerkin(a_vals, a_cols, p_vals):
    row_count, band = a_cols.shape
    width = p_vals.shape[1] // B
    rows_total, groups = lax.axis_size("rows"), lax.axis_size("grp")
    rows_pos, grp_pos = lax.axis_index("rows"), lax.axis_index("grp")
    where = jnp.stack([rows_pos, grp_pos, jnp.int32(groups)]).astype(jnp.int32)
    p_own = p_vals.reshape(row_count * B, width)
    a_own = a_vals.reshape(row_count * B, band * B)

    partner = xor_permute(p_own, "rows", 1)
    onward = [(i, i + 2) for i in range(0, rows_total - 2, 2)]
    onward += [(i, i - 2) for i in range(3, rows_total, 2)]
    beyond = lax.ppermute(partner, "rows", onward)

    p_far, a_far, c_far = (xor_permute(v, "grp", 2) for v in (p_own, a_own, a_cols))
    p_near, a_near, c_near = (xor_permute(v, "grp", 1) for v in (p_own, a_own, a_cols))
    p_last, a_last, c_last = (xor_permute(v, "grp", 1) for v in (p_far, a_far, c_far))

    first = scatter_products(
        where, (a_cols, c_near), (a_own, a_near), (p_own, p_near), band, row_count
    )
    second = scatter_products(
        where, (c_far, c_last), (a_far, a_last), (p_far, p_last), band, row_count
    )
    parts = [
        contract(one, right) + contract(two, right)
        for one, two, right in zip(first, second, (p_own, partner, beyond))
    ]
    stacked = jnp.concatenate(parts, axis=1).reshape(groups, width // groups, 3 * width)
    pieces = lax.all_to_all(stacked, "grp", split_axis=0, concat_axis=0, tiled=True)
    total = jnp.sum(pieces, axis=0).astype(jnp.bfloat16)
    own, direct, diagonal = (total[:, i * width : (i + 1) * width] for i in range(3))
    even = lax.rem(rows_pos, 2) == 0
    return jnp.concatenate(
        [jnp.where(even, diagonal, direct), own, jnp.where(even, direct, diagonal)], axis=1
    )


def local(a_vals, a_cols, p_vals, new_rows):
    coarse = galerkin(a_vals, a_cols, p_vals)
    a_moved = migrate(a_vals, new_rows)
    return (a_moved, coarse)


def solution(mesh):
    in_specs = (
        P(("rows", "grp"), None),
        P(("rows", "grp"), None),
        P(("rows", "grp"), None),
        P(("rows", "grp")),
    )
    out_specs = (P(("rows", "grp"), None), P(("rows", "grp"), None))
    return jax.shard_map(local, mesh=mesh, in_specs=in_specs, out_specs=out_specs, check_vma=False)
```

```python
import functools

import jax
import jax.numpy as jnp
from jax import lax
from jax.experimental import pallas as pl
from jax.experimental.pallas import tpu as pltpu
from jax.sharding import PartitionSpec as P


B = 64
UNROLL = 8
SLOTS = 3


def xor_permute(value, axis, bit):
    count = lax.axis_size(axis)
    return lax.ppermute(value, axis, [(i, i ^ bit) for i in range(count)])


def entry_codes(cols, rows_pos, grp_pos, groups):
    row_count, band = cols.shape
    device = cols // row_count
    near = device // groups - rows_pos
    side = jnp.where(rows_pos % 2 == 1, -near, near)
    slot = jnp.where(near == 0, 0, jnp.where(side == 1, 1, 2))
    target = slot * row_count + cols % row_count
    entry = jnp.arange(row_count, dtype=jnp.int32)[:, None] * band + jnp.arange(
        band, dtype=jnp.int32
    )
    code = entry * target_span(row_count) + target
    return jnp.where(device % groups == grp_pos, code, -1).reshape(-1)


def target_span(row_count):
    return pl.next_power_of_2(SLOTS * row_count + 1)


def clear(sums):
    rows = 2 * B

    def step(i, _):
        sums[pl.ds(pl.multiple_of(i * rows, rows), rows), :] = jnp.zeros(
            (rows, sums.shape[1]), sums.dtype
        )
        return 0

    lax.fori_loop(0, sums.shape[0] // rows, step, 0)


def scatter_part(band, row_count, offset, code_ref, a_ref, p_ref, sums, order):
    entries = row_count * band
    span = target_span(row_count)
    dummy = SLOTS * row_count

    def collect(step, found):
        code = code_ref[offset + step]
        order[found] = code
        return found + jnp.where(code >= 0, 1, 0)

    count = lax.fori_loop(0, entries, collect, 0, unroll=16)
    for pad in range(UNROLL):
        order[count + pad] = dummy

    def batch(step, _):
        terms = []
        for lane in range(UNROLL):
            code = order[step * UNROLL + lane]
            target = jnp.bitwise_and(code, span - 1)
            entry = lax.div(code, span)
            row = lax.div(entry, band)
            k = lax.rem(entry, band)
            start = pl.multiple_of(row * B, B)
            half = pl.multiple_of(lax.div(k, 2) * (2 * B), 2 * B)
            block = a_ref[pl.ds(start, B), pl.ds(half, 2 * B)]
            block = jnp.where(lax.rem(k, 2) == 1, block[:, B:], block[:, :B])
            left = p_ref[pl.ds(start, B), :]
            terms.append((contract(block, left), target))
        for term, target in terms:
            at = pl.ds(pl.multiple_of(target * B, B), B)
            sums[at, :] = sums[at, :] + term
        return 0

    lax.fori_loop(0, lax.div(count + UNROLL - 1, UNROLL), batch, 0)


def contract(left, right):
    return lax.dot_general(
        left, right, (((0,), (0,)), ((), ())), preferred_element_type=jnp.float32
    )


def early_kernel(band, row_count, parts, codes, *refs):
    sources, refs = refs[: 2 * parts], refs[2 * parts :]
    partial, (kept_1, kept_2) = refs[0], refs[1:3]
    buffers, refs = refs[3 : 3 + 2 * parts], refs[3 + 2 * parts :]
    sums, order, sems = refs
    copies = [
        pltpu.make_async_copy(src, dst, sems.at[i])
        for i, (src, dst) in enumerate(zip(sources, buffers))
    ]
    for copy in copies:
        copy.start()
    clear(sums)
    for part in range(parts):
        copies[2 * part].wait()
        copies[2 * part + 1].wait()
        a_ref, p_ref = buffers[2 * part : 2 * part + 2]
        scatter_part(
            band, row_count, part * row_count * band, codes, a_ref, p_ref, sums, order
        )
    size = row_count * B
    partial[...] = contract(sums[:size].astype(jnp.bfloat16), buffers[1][...])
    kept_1[...] = sums[size : 2 * size].astype(jnp.bfloat16)
    kept_2[...] = sums[2 * size : 3 * size].astype(jnp.bfloat16)


def late_kernel(band, row_count, parts, codes, *refs):
    count = 2 * parts + SLOTS + 3
    sources, refs = refs[:count], refs[count:]
    (keep, send), refs = refs[:2], refs[2:]
    buffers, refs = refs[:count], refs[count:]
    sums, order, sems = refs
    grp_pos = codes[parts * row_count * band]
    groups = 4
    share = keep.shape[0] // 2
    copies = [
        pltpu.make_async_copy(src, dst, sems.at[i])
        for i, (src, dst) in enumerate(zip(sources, buffers))
    ]
    for copy in copies:
        copy.start()
    clear(sums)
    for part in range(parts):
        copies[2 * part].wait()
        copies[2 * part + 1].wait()
        a_ref, p_ref = buffers[2 * part : 2 * part + 2]
        scatter_part(
            band, row_count, part * row_count * band, codes, a_ref, p_ref, sums, order
        )
    size = row_count * B
    rest = buffers[2 * parts :]
    rights, earlier, kept = rest[:SLOTS], rest[SLOTS], rest[SLOTS + 1 :]
    for copy in copies[2 * parts :]:
        copy.wait()
    width = rights[0].shape[1]
    for slot in range(SLOTS):
        right = rights[slot][...]
        here = contract(sums[slot * size : (slot + 1) * size].astype(jnp.bfloat16), right)
        if slot == 0:
            here = here + earlier[...]
        else:
            here = here + contract(kept[slot - 1][...], right)
        for block in range(groups):
            piece = here[block * share : (block + 1) * share]
            place = jnp.bitwise_xor(block, grp_pos)
            at = pl.ds(pl.multiple_of(lax.div(place, 2) * share, share), share)
            columns = slice(slot * width, (slot + 1) * width)

            @pl.when(lax.rem(place, 2) == 0)
            def _():
                keep[at, columns] = piece

            @pl.when(lax.rem(place, 2) == 1)
            def _():
                send[at, columns] = piece


def run_products(body, codes, arrays, outs, band, row_count, parts, flops):
    width = arrays[1].shape[1]
    return pl.pallas_call(
        functools.partial(body, band, row_count, parts),
        out_shape=outs,
        in_specs=[pl.BlockSpec(memory_space=pltpu.SMEM)]
        + [pl.BlockSpec(memory_space=pl.ANY)] * len(arrays),
        out_specs=jax.tree.map(lambda _: pl.BlockSpec(memory_space=pltpu.VMEM), outs),
        scratch_shapes=[pltpu.VMEM(x.shape, x.dtype) for x in arrays]
        + [
            pltpu.VMEM(((SLOTS * row_count + 2) * B, width), jnp.float32),
            pltpu.SMEM((row_count * band + UNROLL,), jnp.int32),
            pltpu.SemaphoreType.DMA((len(arrays),)),
        ],
        compiler_params=pltpu.CompilerParams(vmem_limit_bytes=56 << 20),
        cost_estimate=pl.CostEstimate(
            flops=flops,
            bytes_accessed=sum(x.size * x.dtype.itemsize for x in arrays),
            transcendentals=0,
        ),
    )(codes, *arrays)


def galerkin(a_vals, a_cols, p_vals):
    row_count, band = a_cols.shape
    width = p_vals.shape[1] // B
    rows_total, groups = lax.axis_size("rows"), lax.axis_size("grp")
    rows_pos, grp_pos = lax.axis_index("rows"), lax.axis_index("grp")
    assert groups == 4 and rows_total % 2 == 0
    p_own = p_vals.reshape(row_count * B, width)
    a_own = a_vals.reshape(row_count * B, band * B)

    partner = xor_permute(p_own, "rows", 1)
    both = ("rows", "grp")
    ahead = [
        (i * groups + g, j * groups + g)
        for g in range(1, groups, 2)
        for i in range(rows_total)
        for j in [i + 2 if i % 2 else i - 2]
        if 0 <= j < rows_total
    ]
    last = [
        (i * groups + g, j * groups + g)
        for g in range(0, groups, 2)
        for i in range(rows_total)
        for j in [i - 2 if i % 2 else i + 2]
        if 0 <= j < rows_total
    ]
    last += [(i * groups + g, (i ^ 1) * groups + g) for g in range(1, groups, 2) for i in range(rows_total)]
    moved = lax.ppermute(p_own, both, ahead)
    relay = jnp.where(grp_pos % 2 == 0, partner, moved)
    beyond = lax.ppermute(relay, both, last)

    c_far = xor_permute(a_cols, "grp", 2)
    c_near = xor_permute(a_cols, "grp", 1)
    c_last = xor_permute(c_far, "grp", 1)
    p_far = xor_permute(p_own, "grp", 2)
    a_far = xor_permute(a_own, "grp", 2)
    p_near = xor_permute(p_own, "grp", 1)
    a_near = xor_permute(a_own, "grp", 1)
    p_last = xor_permute(p_far, "grp", 1)
    a_last = xor_permute(a_far, "grp", 1)

    def codes(*cols):
        return jnp.concatenate([entry_codes(c, rows_pos, grp_pos, groups) for c in cols])

    flops = 4 * row_count * band * B * B * width // 2
    kept = jax.ShapeDtypeStruct((row_count * B, width), jnp.bfloat16)
    square = jax.ShapeDtypeStruct((width, width), jnp.float32)
    partial, kept_1, kept_2 = run_products(
        early_kernel,
        codes(a_cols, c_near),
        (a_own, p_own, a_near, p_near),
        (square, kept, kept),
        band,
        row_count,
        2,
        flops,
    )
    half = jax.ShapeDtypeStruct((width // 2, SLOTS * width), jnp.float32)
    keep, send = run_products(
        late_kernel,
        jnp.concatenate([codes(c_far, c_last), grp_pos.reshape(1)]),
        (a_far, p_far, a_last, p_last, p_own, partner, beyond, partial, kept_1, kept_2),
        (half, half),
        band,
        row_count,
        2,
        flops,
    )
    share = width // groups
    pair = keep + xor_permute(send, "grp", 1)
    total = pair[:share] + xor_permute(pair[share:], "grp", 2)
    total = total.astype(jnp.bfloat16)
    own, direct, diagonal = (total[:, i * width : (i + 1) * width] for i in range(SLOTS))
    even = rows_pos % 2 == 0
    return jnp.concatenate(
        [jnp.where(even, diagonal, direct), own, jnp.where(even, direct, diagonal)], axis=1
    )


def gather_kernel(chunks, capacity, source, target, probe, buffer, sems_probe, sems_in, sems_out):
    probes = [
        pltpu.make_async_copy(
            source.at[pl.ds(c * capacity, capacity), pl.ds(0, probe.shape[2])],
            probe.at[c],
            sems_probe.at[c],
        )
        for c in range(chunks)
    ]
    for copy in probes:
        copy.start()
    full, place, at = [], [], jnp.int32(0)
    limit = target.shape[0] // capacity - 1
    for c in range(chunks):
        probes[c].wait()
        here = jnp.max(probe[c].astype(jnp.float32)) < jnp.inf
        full.append(here)
        place.append(pl.multiple_of(jnp.minimum(at, limit) * capacity, capacity))
        at = at + jnp.where(here, 1, 0)

    def loads(c):
        return pltpu.make_async_copy(
            source.at[pl.ds(c * capacity, capacity), :],
            buffer.at[pl.ds(place[c], capacity), :],
            sems_in.at[c],
        )

    def stores(c):
        return pltpu.make_async_copy(
            buffer.at[pl.ds(place[c], capacity), :],
            target.at[pl.ds(place[c], capacity), :],
            sems_out.at[c],
        )

    for c in range(chunks):
        @pl.when(full[c])
        def _():
            loads(c).start()

    for c in range(chunks):
        @pl.when(full[c])
        def _():
            loads(c).wait()
            stores(c).start()

    for c in range(chunks):
        @pl.when(full[c])
        def _():
            stores(c).wait()


def gather_chunks(incoming, row_count, chunks, capacity):
    row_width = incoming.shape[1]
    return pl.pallas_call(
        functools.partial(gather_kernel, chunks, capacity),
        out_shape=jax.ShapeDtypeStruct((row_count, row_width), incoming.dtype),
        in_specs=[pl.BlockSpec(memory_space=pl.ANY)],
        out_specs=pl.BlockSpec(memory_space=pl.ANY),
        scratch_shapes=[
            pltpu.VMEM((chunks, capacity, 128), incoming.dtype),
            pltpu.VMEM((row_count, row_width), incoming.dtype),
            pltpu.SemaphoreType.DMA((chunks,)),
            pltpu.SemaphoreType.DMA((chunks,)),
            pltpu.SemaphoreType.DMA((chunks,)),
        ],
        name="gather_chunks",
    )(incoming)


def migrate(a_vals, new_rows):
    row_count, row_width = a_vals.shape
    rows_total = lax.axis_size("rows")
    capacity = max(2, 2 * row_count // rows_total)
    slot_total = rows_total * capacity
    earlier = jnp.arange(row_count)[None, :] < jnp.arange(row_count)[:, None]
    same = new_rows[:, None] == new_rows[None, :]
    ranking = jnp.sum((earlier & same).astype(jnp.int32), axis=1)
    slot_of = new_rows * capacity + ranking
    slot_ids = jnp.arange(slot_total, dtype=jnp.int32)
    sender = slot_ids[:, None] == slot_of[None, :]
    picked = jnp.dot(sender.astype(jnp.bfloat16), a_vals, preferred_element_type=jnp.float32)
    filled = jnp.any(sender, axis=1)
    chunked = capacity % 16 == 0
    if chunked:
        picked = jnp.where(filled[:, None], picked, jnp.inf)
    incoming = lax.all_to_all(
        picked.astype(a_vals.dtype).reshape(rows_total, capacity, row_width),
        "rows",
        split_axis=0,
        concat_axis=0,
        tiled=True,
    ).reshape(slot_total, row_width)
    if chunked:
        return gather_chunks(incoming, row_count, rows_total, capacity)
    flags = lax.all_to_all(
        filled.astype(jnp.bfloat16).reshape(rows_total, capacity),
        "rows",
        split_axis=0,
        concat_axis=0,
        tiled=True,
    )
    flat_flags = flags.reshape(slot_total).astype(jnp.float32)
    position = jnp.cumsum(flat_flags) - 1.0
    wanted = jnp.arange(row_count, dtype=jnp.float32)
    receiver = (position[None, :] == wanted[:, None]) & (flat_flags[None, :] > 0.0)
    return jnp.dot(
        receiver.astype(jnp.bfloat16), incoming, preferred_element_type=jnp.float32
    ).astype(a_vals.dtype)


def local(a_vals, a_cols, p_vals, new_rows):
    a_moved = migrate(a_vals, new_rows)
    coarse = galerkin(a_vals, a_cols, p_vals)
    return (a_moved, coarse)


def solution(mesh):
    in_specs = (
        P(("rows", "grp"), None),
        P(("rows", "grp"), None),
        P(("rows", "grp"), None),
        P(("rows", "grp")),
    )
    out_specs = (P(("rows", "grp"), None), P(("rows", "grp"), None))
    return jax.shard_map(local, mesh=mesh, in_specs=in_specs, out_specs=out_specs, check_vma=False)
```

```python
import functools

import jax
import jax.numpy as jnp
from jax import lax
from jax.experimental import pallas as pl
from jax.experimental.pallas import tpu as pltpu
from jax.sharding import PartitionSpec as P


B = 64
UNROLL = 8
SLOTS = 3


def xor_permute(value, axis, bit):
    count = lax.axis_size(axis)
    return lax.ppermute(value, axis, [(i, i ^ bit) for i in range(count)])


def entry_codes(cols, rows_pos, grp_pos, groups):
    row_count, band = cols.shape
    device = cols // row_count
    near = device // groups - rows_pos
    side = jnp.where(rows_pos % 2 == 1, -near, near)
    slot = jnp.where(near == 0, 0, jnp.where(side == 1, 1, 2))
    target = slot * row_count + cols % row_count
    entry = jnp.arange(row_count, dtype=jnp.int32)[:, None] * band + jnp.arange(
        band, dtype=jnp.int32
    )
    code = entry * target_span(row_count) + target
    return jnp.where(device % groups == grp_pos, code, -1).reshape(-1)


def target_span(row_count):
    return pl.next_power_of_2(SLOTS * row_count + 1)


def clear(sums):
    rows = 2 * B

    def step(i, _):
        sums[pl.ds(pl.multiple_of(i * rows, rows), rows), :] = jnp.zeros(
            (rows, sums.shape[1]), sums.dtype
        )
        return 0

    lax.fori_loop(0, sums.shape[0] // rows, step, 0)


def scatter_part(band, row_count, offset, code_ref, a_ref, p_ref, sums, order):
    entries = row_count * band
    span = target_span(row_count)
    dummy = SLOTS * row_count

    def collect(step, found):
        code = code_ref[offset + step]
        order[found] = code
        return found + jnp.where(code >= 0, 1, 0)

    count = lax.fori_loop(0, entries, collect, 0, unroll=16)
    for pad in range(UNROLL):
        order[count + pad] = dummy

    def batch(step, _):
        terms = []
        for lane in range(UNROLL):
            code = order[step * UNROLL + lane]
            target = jnp.bitwise_and(code, span - 1)
            entry = lax.div(code, span)
            row = lax.div(entry, band)
            k = lax.rem(entry, band)
            start = pl.multiple_of(row * B, B)
            half = pl.multiple_of(lax.div(k, 2) * (2 * B), 2 * B)
            block = a_ref[pl.ds(start, B), pl.ds(half, 2 * B)]
            block = jnp.where(lax.rem(k, 2) == 1, block[:, B:], block[:, :B])
            left = p_ref[pl.ds(start, B), :]
            terms.append((contract(block, left), target))
        for term, target in terms:
            at = pl.ds(pl.multiple_of(target * B, B), B)
            sums[at, :] = sums[at, :] + term
        return 0

    lax.fori_loop(0, lax.div(count + UNROLL - 1, UNROLL), batch, 0)


def contract(left, right):
    return lax.dot_general(
        left, right, (((0,), (0,)), ((), ())), preferred_element_type=jnp.float32
    )


def early_kernel(band, row_count, parts, codes, *refs):
    sources, refs = refs[: 2 * parts], refs[2 * parts :]
    partial, (kept_1, kept_2) = refs[0], refs[1:3]
    buffers, refs = refs[3 : 3 + 2 * parts], refs[3 + 2 * parts :]
    sums, order, sems = refs
    copies = [
        pltpu.make_async_copy(src, dst, sems.at[i])
        for i, (src, dst) in enumerate(zip(sources, buffers))
    ]
    for copy in copies:
        copy.start()
    clear(sums)
    for part in range(parts):
        copies[2 * part].wait()
        copies[2 * part + 1].wait()
        a_ref, p_ref = buffers[2 * part : 2 * part + 2]
        scatter_part(
            band, row_count, part * row_count * band, codes, a_ref, p_ref, sums, order
        )
    size = row_count * B
    partial[...] = contract(sums[:size].astype(jnp.bfloat16), buffers[1][...])
    kept_1[...] = sums[size : 2 * size].astype(jnp.bfloat16)
    kept_2[...] = sums[2 * size : 3 * size].astype(jnp.bfloat16)


def late_kernel(band, row_count, parts, codes, *refs):
    count = 2 * parts + SLOTS + 3
    sources, refs = refs[: count + 1], refs[count + 1 :]
    (keep, send), refs = refs[:2], refs[2:]
    buffers, refs = refs[:count], refs[count:]
    sums, order, sems = refs
    grp_pos = codes[parts * row_count * band]
    groups = 4
    share = keep.shape[0] // 2
    odd_at = 2 * parts + SLOTS
    sources, other = sources[:odd_at] + sources[odd_at + 1 :], sources[odd_at]
    copies = [
        pltpu.make_async_copy(src, dst, sems.at[i])
        for i, (src, dst) in enumerate(zip(sources, buffers))
    ]
    other = pltpu.make_async_copy(other, buffers[odd_at - 1], sems.at[odd_at - 1])
    for i, copy in enumerate(copies):
        if i == odd_at - 1:
            pl.when(lax.rem(grp_pos, 2) == 0)(copy.start)
            pl.when(lax.rem(grp_pos, 2) == 1)(other.start)
        else:
            copy.start()
    clear(sums)
    for part in range(parts):
        copies[2 * part].wait()
        copies[2 * part + 1].wait()
        a_ref, p_ref = buffers[2 * part : 2 * part + 2]
        scatter_part(
            band, row_count, part * row_count * band, codes, a_ref, p_ref, sums, order
        )
    size = row_count * B
    rest = buffers[2 * parts :]
    rights, earlier, kept = rest[:SLOTS], rest[SLOTS], rest[SLOTS + 1 :]
    for copy in copies[2 * parts :]:
        copy.wait()
    width = rights[0].shape[1]
    for slot in range(SLOTS):
        right = rights[slot][...]
        here = contract(sums[slot * size : (slot + 1) * size].astype(jnp.bfloat16), right)
        if slot == 0:
            here = here + earlier[...]
        else:
            here = here + contract(kept[slot - 1][...], right)
        for block in range(groups):
            piece = here[block * share : (block + 1) * share]
            place = jnp.bitwise_xor(block, grp_pos)
            at = pl.ds(pl.multiple_of(lax.div(place, 2) * share, share), share)
            columns = slice(slot * width, (slot + 1) * width)

            @pl.when(lax.rem(place, 2) == 0)
            def _():
                keep[at, columns] = piece

            @pl.when(lax.rem(place, 2) == 1)
            def _():
                send[at, columns] = piece


def run_products(body, codes, arrays, outs, band, row_count, parts, flops, skip=()):
    width = arrays[1].shape[1]
    held = [x for i, x in enumerate(arrays) if i not in skip]
    return pl.pallas_call(
        functools.partial(body, band, row_count, parts),
        out_shape=outs,
        in_specs=[pl.BlockSpec(memory_space=pltpu.SMEM)]
        + [pl.BlockSpec(memory_space=pl.ANY)] * len(arrays),
        out_specs=jax.tree.map(lambda _: pl.BlockSpec(memory_space=pltpu.VMEM), outs),
        scratch_shapes=[pltpu.VMEM(x.shape, x.dtype) for x in held]
        + [
            pltpu.VMEM(((SLOTS * row_count + 2) * B, width), jnp.float32),
            pltpu.SMEM((row_count * band + UNROLL,), jnp.int32),
            pltpu.SemaphoreType.DMA((len(held),)),
        ],
        compiler_params=pltpu.CompilerParams(vmem_limit_bytes=56 << 20),
        cost_estimate=pl.CostEstimate(
            flops=flops,
            bytes_accessed=sum(x.size * x.dtype.itemsize for x in arrays),
            transcendentals=0,
        ),
    )(codes, *arrays)


def galerkin(a_vals, a_cols, p_vals):
    row_count, band = a_cols.shape
    width = p_vals.shape[1] // B
    rows_total, groups = lax.axis_size("rows"), lax.axis_size("grp")
    rows_pos, grp_pos = lax.axis_index("rows"), lax.axis_index("grp")
    assert groups == 4 and rows_total % 2 == 0
    p_own = p_vals.reshape(row_count * B, width)
    a_own = a_vals.reshape(row_count * B, band * B)

    partner = xor_permute(p_own, "rows", 1)
    both = ("rows", "grp")
    ahead = [
        (i * groups + g, j * groups + g)
        for g in range(1, groups, 2)
        for i in range(rows_total)
        for j in [i + 2 if i % 2 else i - 2]
        if 0 <= j < rows_total
    ]
    onward = [
        (i * groups + g, j * groups + g)
        for g in range(0, groups, 2)
        for i in range(rows_total)
        for j in [i - 2 if i % 2 else i + 2]
        if 0 <= j < rows_total
    ]
    across = [
        (i * groups + g, (i ^ 1) * groups + g)
        for g in range(1, groups, 2)
        for i in range(rows_total)
    ]
    moved = lax.ppermute(p_own, both, ahead)
    beyond_even = lax.ppermute(partner, both, onward)
    beyond_odd = lax.ppermute(moved, both, across)

    c_far = xor_permute(a_cols, "grp", 2)
    c_near = xor_permute(a_cols, "grp", 1)
    c_last = xor_permute(c_far, "grp", 1)
    p_far = xor_permute(p_own, "grp", 2)
    a_far = xor_permute(a_own, "grp", 2)
    p_near = xor_permute(p_own, "grp", 1)
    a_near = xor_permute(a_own, "grp", 1)
    p_last = xor_permute(p_far, "grp", 1)
    a_last = xor_permute(a_far, "grp", 1)

    def codes(*cols):
        return jnp.concatenate([entry_codes(c, rows_pos, grp_pos, groups) for c in cols])

    flops = 4 * row_count * band * B * B * width // 2
    kept = jax.ShapeDtypeStruct((row_count * B, width), jnp.bfloat16)
    square = jax.ShapeDtypeStruct((width, width), jnp.float32)
    partial, kept_1, kept_2 = run_products(
        early_kernel,
        codes(a_cols, c_near),
        (a_own, p_own, a_near, p_near),
        (square, kept, kept),
        band,
        row_count,
        2,
        flops,
    )
    half = jax.ShapeDtypeStruct((width // 2, SLOTS * width), jnp.float32)
    keep, send = run_products(
        late_kernel,
        jnp.concatenate([codes(c_far, c_last), grp_pos.reshape(1)]),
        (a_far, p_far, a_last, p_last, p_own, partner, beyond_even, beyond_odd, partial, kept_1, kept_2),
        (half, half),
        band,
        row_count,
        2,
        flops,
        skip=(4 + SLOTS,),
    )
    share = width // groups
    pair = keep + xor_permute(send, "grp", 1)
    total = pair[:share] + xor_permute(pair[share:], "grp", 2)
    total = total.astype(jnp.bfloat16)
    own, direct, diagonal = (total[:, i * width : (i + 1) * width] for i in range(SLOTS))
    even = rows_pos % 2 == 0
    return jnp.concatenate(
        [jnp.where(even, diagonal, direct), own, jnp.where(even, direct, diagonal)], axis=1
    )


def pack_kernel(chunks, capacity, slot_ref, a_ref, *outs):
    slots = chunks * capacity
    hot = lax.broadcasted_iota(jnp.int32, (slots, a_ref.shape[0]), 0) == slot_ref[...]
    hot = hot.astype(jnp.float32)
    filled = jnp.sum(hot, axis=1, keepdims=True) > 0.5
    picked = jnp.dot(
        hot.astype(jnp.bfloat16), a_ref[...], preferred_element_type=jnp.float32
    )
    picked = jnp.where(filled, picked, jnp.inf).astype(jnp.bfloat16)
    for chunk in range(chunks):
        outs[chunk][...] = picked[chunk * capacity : (chunk + 1) * capacity]


def pack_chunks(a_vals, slot_of, chunks, capacity):
    row_count, row_width = a_vals.shape
    columns = 2048
    return pl.pallas_call(
        functools.partial(pack_kernel, chunks, capacity),
        grid=(row_width // columns,),
        out_shape=[jax.ShapeDtypeStruct((capacity, row_width), a_vals.dtype)] * chunks,
        in_specs=[
            pl.BlockSpec((1, row_count), lambda i: (0, 0)),
            pl.BlockSpec((row_count, columns), lambda i: (0, i)),
        ],
        out_specs=[pl.BlockSpec((capacity, columns), lambda i: (0, i))] * chunks,
        name="pack",
    )(slot_of[None, :], a_vals)


def gather_kernel(chunks, capacity, where, *refs):
    sources, (target, probe, buffer, sems_probe, sems_in, sems_out) = refs[:chunks], refs[chunks:]
    probes = [
        pltpu.make_async_copy(
            sources[c].at[:, pl.ds(0, probe.shape[2])], probe.at[c], sems_probe.at[c]
        )
        for c in range(chunks)
    ]
    for copy in probes:
        copy.start()
    full = []
    for c in range(chunks):
        probes[c].wait()
        full.append(jnp.where(jnp.max(probe[c].astype(jnp.float32)) < jnp.inf, 1, 0))
    limit = target.shape[0] // capacity - 1
    place = []
    for c in range(chunks):
        sender = jnp.bitwise_xor(where[0], c)
        ahead = jnp.int32(0)
        for other in range(chunks):
            first = jnp.bitwise_xor(where[0], other) < sender
            ahead = ahead + jnp.where(first, full[other], 0)
        place.append(pl.multiple_of(jnp.minimum(ahead, limit) * capacity, capacity))

    def loads(c):
        return pltpu.make_async_copy(
            sources[c], buffer.at[pl.ds(place[c], capacity), :], sems_in.at[c]
        )

    def stores(c):
        return pltpu.make_async_copy(
            buffer.at[pl.ds(place[c], capacity), :],
            target.at[pl.ds(place[c], capacity), :],
            sems_out.at[c],
        )

    for c in range(chunks):
        pl.when(full[c] == 1)(lambda c=c: loads(c).start())
    for c in range(chunks):
        @pl.when(full[c] == 1)
        def _():
            loads(c).wait()
            stores(c).start()

    for c in range(chunks):
        pl.when(full[c] == 1)(lambda c=c: stores(c).wait())


def gather_chunks(incoming, rows_pos, row_count):
    chunks = len(incoming)
    capacity, row_width = incoming[0].shape
    dtype = incoming[0].dtype
    return pl.pallas_call(
        functools.partial(gather_kernel, chunks, capacity),
        out_shape=jax.ShapeDtypeStruct((row_count, row_width), dtype),
        in_specs=[pl.BlockSpec(memory_space=pltpu.SMEM)]
        + [pl.BlockSpec(memory_space=pl.ANY)] * chunks,
        out_specs=pl.BlockSpec(memory_space=pl.ANY),
        scratch_shapes=[
            pltpu.VMEM((chunks, capacity, 128), dtype),
            pltpu.VMEM((row_count, row_width), dtype),
            pltpu.SemaphoreType.DMA((chunks,)),
            pltpu.SemaphoreType.DMA((chunks,)),
            pltpu.SemaphoreType.DMA((chunks,)),
        ],
        name="gather_chunks",
    )(rows_pos.astype(jnp.int32).reshape(1), *incoming)


def use_chunks(row_count, rows_total):
    capacity = max(2, 2 * row_count // rows_total)
    return capacity % 16 == 0 and rows_total & (rows_total - 1) == 0


def migrate(a_vals, new_rows):
    row_count, row_width = a_vals.shape
    rows_total = lax.axis_size("rows")
    capacity = max(2, 2 * row_count // rows_total)
    slot_total = rows_total * capacity
    earlier = jnp.arange(row_count)[None, :] < jnp.arange(row_count)[:, None]
    same = new_rows[:, None] == new_rows[None, :]
    ranking = jnp.sum((earlier & same).astype(jnp.int32), axis=1)
    if use_chunks(row_count, rows_total):
        rows_pos = lax.axis_index("rows")
        slot_of = jnp.bitwise_xor(new_rows, rows_pos) * capacity + ranking
        chunks = pack_chunks(a_vals, slot_of, rows_total, capacity)
        incoming = [chunks[0]] + [
            xor_permute(chunks[bit], "rows", bit)
            for bit in range(1, rows_total)
        ]
        return gather_chunks(incoming, rows_pos, row_count)
    slot_of = new_rows * capacity + ranking
    slot_ids = jnp.arange(slot_total, dtype=jnp.int32)
    sender = slot_ids[:, None] == slot_of[None, :]
    picked = jnp.dot(sender.astype(jnp.bfloat16), a_vals, preferred_element_type=jnp.float32)
    filled = jnp.any(sender, axis=1)
    incoming = lax.all_to_all(
        picked.astype(a_vals.dtype).reshape(rows_total, capacity, row_width),
        "rows",
        split_axis=0,
        concat_axis=0,
        tiled=True,
    ).reshape(slot_total, row_width)
    flags = lax.all_to_all(
        filled.astype(jnp.bfloat16).reshape(rows_total, capacity),
        "rows",
        split_axis=0,
        concat_axis=0,
        tiled=True,
    )
    flat_flags = flags.reshape(slot_total).astype(jnp.float32)
    position = jnp.cumsum(flat_flags) - 1.0
    wanted = jnp.arange(row_count, dtype=jnp.float32)
    receiver = (position[None, :] == wanted[:, None]) & (flat_flags[None, :] > 0.0)
    return jnp.dot(
        receiver.astype(jnp.bfloat16), incoming, preferred_element_type=jnp.float32
    ).astype(a_vals.dtype)


def local(a_vals, a_cols, p_vals, new_rows):
    a_moved = migrate(a_vals, new_rows)
    coarse = galerkin(a_vals, a_cols, p_vals)
    return (a_moved, coarse)


def solution(mesh):
    in_specs = (
        P(("rows", "grp"), None),
        P(("rows", "grp"), None),
        P(("rows", "grp"), None),
        P(("rows", "grp")),
    )
    out_specs = (P(("rows", "grp"), None), P(("rows", "grp"), None))
    return jax.shard_map(local, mesh=mesh, in_specs=in_specs, out_specs=out_specs, check_vma=False)
```

```python
import functools

import jax
import jax.numpy as jnp
from jax import lax
from jax.experimental import pallas as pl
from jax.experimental.pallas import tpu as pltpu
from jax.sharding import PartitionSpec as P


B = 64
UNROLL = 8
SLOTS = 3


def xor_permute(value, axis, bit):
    count = lax.axis_size(axis)
    return lax.ppermute(value, axis, [(i, i ^ bit) for i in range(count)])


def entry_codes(cols, rows_pos, grp_pos, groups):
    row_count, band = cols.shape
    device = cols // row_count
    near = device // groups - rows_pos
    side = jnp.where(rows_pos % 2 == 1, -near, near)
    slot = jnp.where(near == 0, 0, jnp.where(side == 1, 1, 2))
    target = slot * row_count + cols % row_count
    entry = jnp.arange(row_count, dtype=jnp.int32)[:, None] * band + jnp.arange(
        band, dtype=jnp.int32
    )
    code = entry * target_span(row_count) + target
    return jnp.where(device % groups == grp_pos, code, -1).reshape(-1)


def target_span(row_count):
    return pl.next_power_of_2(SLOTS * row_count + 1)


def clear(sums):
    rows = 2 * B

    def step(i, _):
        sums[pl.ds(pl.multiple_of(i * rows, rows), rows), :] = jnp.zeros(
            (rows, sums.shape[1]), sums.dtype
        )
        return 0

    lax.fori_loop(0, sums.shape[0] // rows, step, 0)


def scatter_part(band, row_count, offset, code_ref, a_ref, p_ref, sums, order):
    entries = row_count * band
    span = target_span(row_count)
    dummy = SLOTS * row_count

    def collect(step, found):
        code = code_ref[offset + step]
        order[found] = code
        return found + jnp.where(code >= 0, 1, 0)

    count = lax.fori_loop(0, entries, collect, 0, unroll=16)
    for pad in range(UNROLL):
        order[count + pad] = dummy

    def batch(step, _):
        terms = []
        for lane in range(UNROLL):
            code = order[step * UNROLL + lane]
            target = jnp.bitwise_and(code, span - 1)
            entry = lax.div(code, span)
            row = lax.div(entry, band)
            k = lax.rem(entry, band)
            start = pl.multiple_of(row * B, B)
            half = pl.multiple_of(lax.div(k, 2) * (2 * B), 2 * B)
            block = a_ref[pl.ds(start, B), pl.ds(half, 2 * B)]
            block = jnp.where(lax.rem(k, 2) == 1, block[:, B:], block[:, :B])
            left = p_ref[pl.ds(start, B), :]
            terms.append((contract(block, left), target))
        for term, target in terms:
            at = pl.ds(pl.multiple_of(target * B, B), B)
            sums[at, :] = sums[at, :] + term
        return 0

    lax.fori_loop(0, lax.div(count + UNROLL - 1, UNROLL), batch, 0)


def contract(left, right):
    return lax.dot_general(
        left, right, (((0,), (0,)), ((), ())), preferred_element_type=jnp.float32
    )


def early_kernel(band, row_count, parts, codes, *refs):
    sources, refs = refs[: 2 * parts], refs[2 * parts :]
    partial, (kept_1, kept_2) = refs[0], refs[1:3]
    buffers, refs = refs[3 : 3 + 2 * parts], refs[3 + 2 * parts :]
    sums, order, sems = refs
    copies = [
        pltpu.make_async_copy(src, dst, sems.at[i])
        for i, (src, dst) in enumerate(zip(sources, buffers))
    ]
    for copy in copies:
        copy.start()
    clear(sums)
    for part in range(parts):
        copies[2 * part].wait()
        copies[2 * part + 1].wait()
        a_ref, p_ref = buffers[2 * part : 2 * part + 2]
        scatter_part(
            band, row_count, part * row_count * band, codes, a_ref, p_ref, sums, order
        )
    size = row_count * B
    partial[...] = contract(sums[:size].astype(jnp.bfloat16), buffers[1][...])
    kept_1[...] = sums[size : 2 * size].astype(jnp.bfloat16)
    kept_2[...] = sums[2 * size : 3 * size].astype(jnp.bfloat16)


def late_kernel(band, row_count, parts, codes, *refs):
    count = 2 * parts + SLOTS + 3
    sources, refs = refs[: count + 1], refs[count + 1 :]
    (keep, send), refs = refs[:2], refs[2:]
    buffers, refs = refs[:count], refs[count:]
    sums, order, sems = refs
    grp_pos = codes[parts * row_count * band]
    groups = 4
    share = keep.shape[0] // 2
    odd_at = 2 * parts + SLOTS
    sources, other = sources[:odd_at] + sources[odd_at + 1 :], sources[odd_at]
    copies = [
        pltpu.make_async_copy(src, dst, sems.at[i])
        for i, (src, dst) in enumerate(zip(sources, buffers))
    ]
    other = pltpu.make_async_copy(other, buffers[odd_at - 1], sems.at[odd_at - 1])
    for i, copy in enumerate(copies):
        if i == odd_at - 1:
            pl.when(lax.rem(grp_pos, 2) == 0)(copy.start)
            pl.when(lax.rem(grp_pos, 2) == 1)(other.start)
        else:
            copy.start()
    clear(sums)
    for part in range(parts):
        copies[2 * part].wait()
        copies[2 * part + 1].wait()
        a_ref, p_ref = buffers[2 * part : 2 * part + 2]
        scatter_part(
            band, row_count, part * row_count * band, codes, a_ref, p_ref, sums, order
        )
    size = row_count * B
    rest = buffers[2 * parts :]
    rights, earlier, kept = rest[:SLOTS], rest[SLOTS], rest[SLOTS + 1 :]
    for copy in copies[2 * parts :]:
        copy.wait()
    width = rights[0].shape[1]
    for slot in range(SLOTS):
        right = rights[slot][...]
        here = contract(sums[slot * size : (slot + 1) * size].astype(jnp.bfloat16), right)
        if slot == 0:
            here = here + earlier[...]
        else:
            here = here + contract(kept[slot - 1][...], right)
        for block in range(groups):
            piece = here[block * share : (block + 1) * share]
            place = jnp.bitwise_xor(block, grp_pos)
            at = pl.ds(pl.multiple_of(lax.div(place, 2) * share, share), share)
            columns = slice(slot * width, (slot + 1) * width)

            @pl.when(lax.rem(place, 2) == 0)
            def _():
                keep[at, columns] = piece

            @pl.when(lax.rem(place, 2) == 1)
            def _():
                send[at, columns] = piece


def run_products(body, codes, arrays, outs, band, row_count, parts, flops, skip=()):
    width = arrays[1].shape[1]
    held = [x for i, x in enumerate(arrays) if i not in skip]
    return pl.pallas_call(
        functools.partial(body, band, row_count, parts),
        out_shape=outs,
        in_specs=[pl.BlockSpec(memory_space=pltpu.SMEM)]
        + [pl.BlockSpec(memory_space=pl.ANY)] * len(arrays),
        out_specs=jax.tree.map(lambda _: pl.BlockSpec(memory_space=pltpu.VMEM), outs),
        scratch_shapes=[pltpu.VMEM(x.shape, x.dtype) for x in held]
        + [
            pltpu.VMEM(((SLOTS * row_count + 2) * B, width), jnp.float32),
            pltpu.SMEM((row_count * band + UNROLL,), jnp.int32),
            pltpu.SemaphoreType.DMA((len(held),)),
        ],
        compiler_params=pltpu.CompilerParams(vmem_limit_bytes=56 << 20),
        cost_estimate=pl.CostEstimate(
            flops=flops,
            bytes_accessed=sum(x.size * x.dtype.itemsize for x in arrays),
            transcendentals=0,
        ),
    )(codes, *arrays)


def galerkin(a_vals, a_cols, p_vals):
    row_count, band = a_cols.shape
    width = p_vals.shape[1] // B
    rows_total, groups = lax.axis_size("rows"), lax.axis_size("grp")
    rows_pos, grp_pos = lax.axis_index("rows"), lax.axis_index("grp")
    assert groups == 4 and rows_total % 2 == 0
    p_own = p_vals.reshape(row_count * B, width)
    a_own = a_vals.reshape(row_count * B, band * B)

    partner = xor_permute(p_own, "rows", 1)
    both = ("rows", "grp")
    ahead = [
        (i * groups + g, j * groups + g)
        for g in range(1, groups, 2)
        for i in range(rows_total)
        for j in [i + 2 if i % 2 else i - 2]
        if 0 <= j < rows_total
    ]
    onward = [
        (i * groups + g, j * groups + g)
        for g in range(0, groups, 2)
        for i in range(rows_total)
        for j in [i - 2 if i % 2 else i + 2]
        if 0 <= j < rows_total
    ]
    across = [
        (i * groups + g, (i ^ 1) * groups + g)
        for g in range(1, groups, 2)
        for i in range(rows_total)
    ]
    moved = lax.ppermute(p_own, both, ahead)
    beyond_even = lax.ppermute(partner, both, onward)
    beyond_odd = lax.ppermute(moved, both, across)

    c_far = xor_permute(a_cols, "grp", 2)
    c_near = xor_permute(a_cols, "grp", 1)
    c_last = xor_permute(c_far, "grp", 1)
    p_far = xor_permute(p_own, "grp", 2)
    a_far = xor_permute(a_own, "grp", 2)
    p_near = xor_permute(p_own, "grp", 1)
    a_near = xor_permute(a_own, "grp", 1)
    p_last = xor_permute(p_far, "grp", 1)
    a_last = xor_permute(a_far, "grp", 1)

    def codes(*cols):
        return jnp.concatenate([entry_codes(c, rows_pos, grp_pos, groups) for c in cols])

    flops = 4 * row_count * band * B * B * width // 2
    kept = jax.ShapeDtypeStruct((row_count * B, width), jnp.bfloat16)
    square = jax.ShapeDtypeStruct((width, width), jnp.float32)
    partial, kept_1, kept_2 = run_products(
        early_kernel,
        codes(a_cols, c_near),
        (a_own, p_own, a_near, p_near),
        (square, kept, kept),
        band,
        row_count,
        2,
        flops,
    )
    half = jax.ShapeDtypeStruct((width // 2, SLOTS * width), jnp.float32)
    keep, send = run_products(
        late_kernel,
        jnp.concatenate([codes(c_far, c_last), grp_pos.reshape(1)]),
        (a_far, p_far, a_last, p_last, p_own, partner, beyond_even, beyond_odd, partial, kept_1, kept_2),
        (half, half),
        band,
        row_count,
        2,
        flops,
        skip=(4 + SLOTS,),
    )
    share = width // groups
    pair = keep + xor_permute(send, "grp", 1)
    total = pair[:share] + xor_permute(pair[share:], "grp", 2)
    total = total.astype(jnp.bfloat16)
    own, direct, diagonal = (total[:, i * width : (i + 1) * width] for i in range(SLOTS))
    even = rows_pos % 2 == 0
    return jnp.concatenate(
        [jnp.where(even, diagonal, direct), own, jnp.where(even, direct, diagonal)], axis=1
    )


def pack_kernel(chunks, capacity, slot_ref, a_ref, *outs):
    slots = chunks * capacity
    hot = lax.broadcasted_iota(jnp.int32, (slots, a_ref.shape[0]), 0) == slot_ref[...]
    hot = hot.astype(jnp.float32)
    picked = jnp.dot(
        hot.astype(jnp.bfloat16), a_ref[...], preferred_element_type=jnp.float32
    ).astype(jnp.bfloat16)
    for chunk in range(chunks):
        outs[chunk][...] = picked[chunk * capacity : (chunk + 1) * capacity]

    @pl.when(pl.program_id(0) == 0)
    def _():
        empty = jnp.sum(hot, axis=1, keepdims=True) < 0.5
        marked = jnp.where(empty, jnp.inf, picked[:, :128].astype(jnp.float32))
        marked = marked.astype(jnp.bfloat16)
        for chunk in range(chunks):
            outs[chunk][:, :128] = marked[chunk * capacity : (chunk + 1) * capacity]


def pack_chunks(a_vals, slot_of, chunks, capacity):
    row_count, row_width = a_vals.shape
    columns = 2048
    return pl.pallas_call(
        functools.partial(pack_kernel, chunks, capacity),
        grid=(row_width // columns,),
        out_shape=[jax.ShapeDtypeStruct((capacity, row_width), a_vals.dtype)] * chunks,
        in_specs=[
            pl.BlockSpec((1, row_count), lambda i: (0, 0)),
            pl.BlockSpec((row_count, columns), lambda i: (0, i)),
        ],
        out_specs=[pl.BlockSpec((capacity, columns), lambda i: (0, i))] * chunks,
        name="pack",
    )(slot_of[None, :], a_vals)


def gather_kernel(chunks, capacity, where, *refs):
    sources, (target, probe, buffer, sems_probe, sems_in, sems_out) = refs[:chunks], refs[chunks:]
    probes = [
        pltpu.make_async_copy(
            sources[c].at[:, pl.ds(0, probe.shape[2])], probe.at[c], sems_probe.at[c]
        )
        for c in range(chunks)
    ]
    for copy in probes:
        copy.start()
    full = []
    for c in range(chunks):
        probes[c].wait()
        full.append(jnp.where(jnp.max(probe[c].astype(jnp.float32)) < jnp.inf, 1, 0))
    limit = target.shape[0] // capacity - 1
    place = []
    for c in range(chunks):
        sender = jnp.bitwise_xor(where[0], c)
        ahead = jnp.int32(0)
        for other in range(chunks):
            first = jnp.bitwise_xor(where[0], other) < sender
            ahead = ahead + jnp.where(first, full[other], 0)
        place.append(pl.multiple_of(jnp.minimum(ahead, limit) * capacity, capacity))

    def loads(c):
        return pltpu.make_async_copy(
            sources[c], buffer.at[pl.ds(place[c], capacity), :], sems_in.at[c]
        )

    def stores(c):
        return pltpu.make_async_copy(
            buffer.at[pl.ds(place[c], capacity), :],
            target.at[pl.ds(place[c], capacity), :],
            sems_out.at[c],
        )

    for c in range(chunks):
        pl.when(full[c] == 1)(lambda c=c: loads(c).start())
    for c in range(chunks):
        @pl.when(full[c] == 1)
        def _():
            loads(c).wait()
            stores(c).start()

    for c in range(chunks):
        pl.when(full[c] == 1)(lambda c=c: stores(c).wait())


def gather_chunks(incoming, rows_pos, row_count):
    chunks = len(incoming)
    capacity, row_width = incoming[0].shape
    dtype = incoming[0].dtype
    return pl.pallas_call(
        functools.partial(gather_kernel, chunks, capacity),
        out_shape=jax.ShapeDtypeStruct((row_count, row_width), dtype),
        in_specs=[pl.BlockSpec(memory_space=pltpu.SMEM)]
        + [pl.BlockSpec(memory_space=pl.ANY)] * chunks,
        out_specs=pl.BlockSpec(memory_space=pl.ANY),
        scratch_shapes=[
            pltpu.VMEM((chunks, capacity, 128), dtype),
            pltpu.VMEM((row_count, row_width), dtype),
            pltpu.SemaphoreType.DMA((chunks,)),
            pltpu.SemaphoreType.DMA((chunks,)),
            pltpu.SemaphoreType.DMA((chunks,)),
        ],
        name="gather_chunks",
    )(rows_pos.astype(jnp.int32).reshape(1), *incoming)


def use_chunks(row_count, rows_total):
    capacity = max(2, 2 * row_count // rows_total)
    return capacity % 16 == 0 and rows_total & (rows_total - 1) == 0


def migrate(a_vals, new_rows):
    row_count, row_width = a_vals.shape
    rows_total = lax.axis_size("rows")
    capacity = max(2, 2 * row_count // rows_total)
    slot_total = rows_total * capacity
    earlier = jnp.arange(row_count)[None, :] < jnp.arange(row_count)[:, None]
    same = new_rows[:, None] == new_rows[None, :]
    ranking = jnp.sum((earlier & same).astype(jnp.int32), axis=1)
    if use_chunks(row_count, rows_total):
        rows_pos = lax.axis_index("rows")
        slot_of = jnp.bitwise_xor(new_rows, rows_pos) * capacity + ranking
        chunks = pack_chunks(a_vals, slot_of, rows_total, capacity)
        incoming = [chunks[0]] + [
            xor_permute(chunks[bit], "rows", bit)
            for bit in range(1, rows_total)
        ]
        return gather_chunks(incoming, rows_pos, row_count)
    slot_of = new_rows * capacity + ranking
    slot_ids = jnp.arange(slot_total, dtype=jnp.int32)
    sender = slot_ids[:, None] == slot_of[None, :]
    picked = jnp.dot(sender.astype(jnp.bfloat16), a_vals, preferred_element_type=jnp.float32)
    filled = jnp.any(sender, axis=1)
    incoming = lax.all_to_all(
        picked.astype(a_vals.dtype).reshape(rows_total, capacity, row_width),
        "rows",
        split_axis=0,
        concat_axis=0,
        tiled=True,
    ).reshape(slot_total, row_width)
    flags = lax.all_to_all(
        filled.astype(jnp.bfloat16).reshape(rows_total, capacity),
        "rows",
        split_axis=0,
        concat_axis=0,
        tiled=True,
    )
    flat_flags = flags.reshape(slot_total).astype(jnp.float32)
    position = jnp.cumsum(flat_flags) - 1.0
    wanted = jnp.arange(row_count, dtype=jnp.float32)
    receiver = (position[None, :] == wanted[:, None]) & (flat_flags[None, :] > 0.0)
    return jnp.dot(
        receiver.astype(jnp.bfloat16), incoming, preferred_element_type=jnp.float32
    ).astype(a_vals.dtype)


def local(a_vals, a_cols, p_vals, new_rows):
    a_moved = migrate(a_vals, new_rows)
    coarse = galerkin(a_vals, a_cols, p_vals)
    return (a_moved, coarse)


def solution(mesh):
    in_specs = (
        P(("rows", "grp"), None),
        P(("rows", "grp"), None),
        P(("rows", "grp"), None),
        P(("rows", "grp")),
    )
    out_specs = (P(("rows", "grp"), None), P(("rows", "grp"), None))
    return jax.shard_map(local, mesh=mesh, in_specs=in_specs, out_specs=out_specs, check_vma=False)
```

```python
import functools

import jax
import jax.numpy as jnp
from jax import lax
from jax.experimental import pallas as pl
from jax.experimental.pallas import tpu as pltpu
from jax.sharding import PartitionSpec as P


B = 64
UNROLL = 8
SLOTS = 3


def xor_permute(value, axis, bit):
    count = lax.axis_size(axis)
    return lax.ppermute(value, axis, [(i, i ^ bit) for i in range(count)])


def entry_codes(cols, rows_pos, grp_pos, groups):
    row_count, band = cols.shape
    device = cols // row_count
    near = device // groups - rows_pos
    side = jnp.where(rows_pos % 2 == 1, -near, near)
    slot = jnp.where(near == 0, 0, jnp.where(side == 1, 1, 2))
    target = slot * row_count + cols % row_count
    entry = jnp.arange(row_count, dtype=jnp.int32)[:, None] * band + jnp.arange(
        band, dtype=jnp.int32
    )
    code = entry * target_span(row_count) + target
    return jnp.where(device % groups == grp_pos, code, -1).reshape(-1)


def target_span(row_count):
    return pl.next_power_of_2(SLOTS * row_count + 1)


def clear(sums):
    rows = 2 * B

    def step(i, _):
        sums[pl.ds(pl.multiple_of(i * rows, rows), rows), :] = jnp.zeros(
            (rows, sums.shape[1]), sums.dtype
        )
        return 0

    lax.fori_loop(0, sums.shape[0] // rows, step, 0)


def scatter_part(band, row_count, offset, base, code_ref, a_ref, p_ref, sums, order):
    entries = a_ref.shape[0] // B * band
    span = target_span(row_count)
    dummy = base * band * span + SLOTS * row_count

    def collect(step, found):
        code = code_ref[offset + base * band + step]
        order[found] = code
        return found + jnp.where(code >= 0, 1, 0)

    count = lax.fori_loop(0, entries, collect, 0, unroll=16)
    for pad in range(UNROLL):
        order[count + pad] = dummy

    def batch(step, _):
        terms = []
        for lane in range(UNROLL):
            code = order[step * UNROLL + lane]
            target = jnp.bitwise_and(code, span - 1)
            entry = lax.div(code, span)
            row = lax.div(entry, band) - base
            k = lax.rem(entry, band)
            start = pl.multiple_of(row * B, B)
            half = pl.multiple_of(lax.div(k, 2) * (2 * B), 2 * B)
            block = a_ref[pl.ds(start, B), pl.ds(half, 2 * B)]
            block = jnp.where(lax.rem(k, 2) == 1, block[:, B:], block[:, :B])
            left = p_ref[pl.ds(start, B), :]
            terms.append((contract(block, left), target))
        for term, target in terms:
            at = pl.ds(pl.multiple_of(target * B, B), B)
            sums[at, :] = sums[at, :] + term
        return 0

    lax.fori_loop(0, lax.div(count + UNROLL - 1, UNROLL), batch, 0)


def contract(left, right):
    return lax.dot_general(
        left, right, (((0,), (0,)), ((), ())), preferred_element_type=jnp.float32
    )


def copies_of(loads, sources, buffers, sems, parity):
    copies = []
    for i, (source, start, buffer, at, rows, when) in enumerate(loads):
        copy = pltpu.make_async_copy(
            sources[source].at[pl.ds(start, rows), :],
            buffers[buffer].at[pl.ds(at, rows), :],
            sems.at[i],
        )
        copies.append((copy, when))
        if when is None:
            copy.start()
        else:
            pl.when(parity == when)(copy.start)

    def wait(i):
        copy, when = copies[i]
        if when is None:
            copy.wait()
        else:
            pl.when(parity == when)(copy.wait)

    return wait


def early_kernel(band, row_count, loads, inputs, codes, *refs):
    sources, (partial, kept_1, kept_2), refs = refs[:inputs], refs[inputs : inputs + 3], refs[inputs + 3 :]
    buffers, (sums, order, sems) = refs[:-3], refs[-3:]
    wait = copies_of(loads, sources, buffers, sems, None)
    clear(sums)
    for part in range(2):
        for i in range(3):
            wait(3 * part + i)
        a_ref, p_ref = buffers[2 * part : 2 * part + 2]
        scatter_part(
            band, row_count, part * row_count * band, 0, codes, a_ref, p_ref, sums, order
        )
    size = row_count * B
    partial[...] = contract(sums[:size].astype(jnp.bfloat16), buffers[1][...])
    kept_1[...] = sums[size : 2 * size].astype(jnp.bfloat16)
    kept_2[...] = sums[2 * size : 3 * size].astype(jnp.bfloat16)


def later_sums(band, row_count, base, wait, codes, buffers, sums, order):
    clear(sums)
    for part in range(2):
        wait(2 * part)
        wait(2 * part + 1)
        a_ref, p_ref = buffers[2 * part : 2 * part + 2]
        scatter_part(
            band, row_count, part * row_count * band, base, codes, a_ref, p_ref, sums, order
        )


def mid_kernel(band, row_count, loads, inputs, codes, *refs):
    sources, result, refs = refs[:inputs], refs[inputs], refs[inputs + 1 :]
    buffers, (sums, order, sems) = refs[:-3], refs[-3:]
    parity = lax.rem(codes[2 * row_count * band], 2)
    wait = copies_of(loads, sources, buffers, sems, parity)
    later_sums(band, row_count, 0, wait, codes, buffers, sums, order)
    for i in range(4, len(loads)):
        wait(i)
    size = row_count * B
    rights, partial, kept = buffers[4 : 4 + SLOTS], buffers[4 + SLOTS], buffers[5 + SLOTS :]
    width = partial.shape[1]
    for slot in range(SLOTS):
        right = rights[slot][...]
        here = contract(sums[slot * size : (slot + 1) * size].astype(jnp.bfloat16), right)
        if slot == 0:
            here = here + partial[...]
        else:
            here = here + contract(kept[slot - 1][...], right)
        result[:, slot * width : (slot + 1) * width] = here


def late_kernel(band, row_count, loads, inputs, codes, *refs):
    sources, (keep, send), refs = refs[:inputs], refs[inputs : inputs + 2], refs[inputs + 2 :]
    buffers, (sums, order, sems) = refs[:-3], refs[-3:]
    grp_pos = codes[2 * row_count * band]
    wait = copies_of(loads, sources, buffers, sems, lax.rem(grp_pos, 2))
    later_sums(band, row_count, row_count // 2, wait, codes, buffers, sums, order)
    for i in range(4, len(loads)):
        wait(i)
    size = row_count * B
    rights, earlier = buffers[4 : 4 + SLOTS], buffers[4 + SLOTS]
    width = rights[0].shape[1]
    share = keep.shape[0] // 2
    for slot in range(SLOTS):
        columns = slice(slot * width, (slot + 1) * width)
        here = contract(
            sums[slot * size : (slot + 1) * size].astype(jnp.bfloat16), rights[slot][...]
        )
        here = here + earlier[:, columns]
        for block in range(width // share):
            piece = here[block * share : (block + 1) * share]
            place = jnp.bitwise_xor(block, grp_pos)
            at = pl.ds(pl.multiple_of(lax.div(place, 2) * share, share), share)

            @pl.when(lax.rem(place, 2) == 0)
            def _():
                keep[at, columns] = piece

            @pl.when(lax.rem(place, 2) == 1)
            def _():
                send[at, columns] = piece


def run_products(body, codes, arrays, loads, buffers, outs, band, row_count, flops):
    width = arrays[0].shape[1]
    held = sum(x.size * x.dtype.itemsize for x in buffers) + SLOTS * row_count * B * width * 4
    return pl.pallas_call(
        functools.partial(body, band, row_count, loads, len(arrays)),
        out_shape=outs,
        in_specs=[pl.BlockSpec(memory_space=pltpu.SMEM)]
        + [pl.BlockSpec(memory_space=pl.ANY)] * len(arrays),
        out_specs=jax.tree.map(lambda _: pl.BlockSpec(memory_space=pltpu.VMEM), outs),
        scratch_shapes=[pltpu.VMEM(x.shape, x.dtype) for x in buffers]
        + [
            pltpu.VMEM(((SLOTS * row_count + 2) * B, width), jnp.float32),
            pltpu.SMEM((row_count * band + UNROLL,), jnp.int32),
            pltpu.SemaphoreType.DMA((len(loads),)),
        ],
        compiler_params=pltpu.CompilerParams(vmem_limit_bytes=held + (16 << 20)),
        cost_estimate=pl.CostEstimate(
            flops=flops,
            bytes_accessed=sum(x.size * x.dtype.itemsize for x in arrays),
            transcendentals=0,
        ),
    )(codes, *arrays)


def galerkin(a_vals, a_cols, p_vals):
    row_count, band = a_cols.shape
    width = p_vals.shape[1] // B
    rows_total, groups = lax.axis_size("rows"), lax.axis_size("grp")
    rows_pos, grp_pos = lax.axis_index("rows"), lax.axis_index("grp")
    assert groups == 4 and rows_total % 2 == 0
    p_own = p_vals.reshape(row_count * B, width)
    cut = row_count // 2
    a_own = [a_vals[i * cut : (i + 1) * cut].reshape(cut * B, band * B) for i in range(2)]

    partner = xor_permute(p_own, "rows", 1)
    both = ("rows", "grp")
    ahead = [
        (i * groups + g, j * groups + g)
        for g in range(1, groups, 2)
        for i in range(rows_total)
        for j in [i + 2 if i % 2 else i - 2]
        if 0 <= j < rows_total
    ]
    onward = [
        (i * groups + g, j * groups + g)
        for g in range(0, groups, 2)
        for i in range(rows_total)
        for j in [i - 2 if i % 2 else i + 2]
        if 0 <= j < rows_total
    ]
    across = [
        (i * groups + g, (i ^ 1) * groups + g)
        for g in range(1, groups, 2)
        for i in range(rows_total)
    ]
    moved = lax.ppermute(p_own, both, ahead)
    beyond_even = lax.ppermute(partner, both, onward)
    beyond_odd = lax.ppermute(moved, both, across)

    c_far = xor_permute(a_cols, "grp", 2)
    c_near = xor_permute(a_cols, "grp", 1)
    c_last = xor_permute(c_far, "grp", 1)
    p_far = xor_permute(p_own, "grp", 2)
    p_near = xor_permute(p_own, "grp", 1)
    p_last = xor_permute(p_far, "grp", 1)
    a_far = [xor_permute(a_own[i], "grp", 2) for i in range(2)]
    a_near = [xor_permute(a_own[i], "grp", 1) for i in range(2)]
    a_last = [xor_permute(a_far[i], "grp", 1) for i in range(2)]

    def codes(*cols):
        return [entry_codes(c, rows_pos, grp_pos, groups) for c in cols]

    flops = 4 * row_count * band * B * B * width // 2
    full, part = row_count * B, cut * B
    whole = jax.ShapeDtypeStruct((full, width), jnp.bfloat16)
    piece = jax.ShapeDtypeStruct((part, width), jnp.bfloat16)
    square = jax.ShapeDtypeStruct((width, width), jnp.float32)
    wide = jax.ShapeDtypeStruct((width, SLOTS * width), jnp.float32)
    half = jax.ShapeDtypeStruct((width // 2, SLOTS * width), jnp.float32)
    partial, kept_1, kept_2 = run_products(
        early_kernel,
        jnp.concatenate(codes(a_cols, c_near)),
        (*a_own, p_own, *a_near, p_near),
        [
            (0, 0, 0, 0, part, None),
            (1, 0, 0, part, part, None),
            (2, 0, 1, 0, full, None),
            (3, 0, 2, 0, part, None),
            (4, 0, 2, part, part, None),
            (5, 0, 3, 0, full, None),
        ],
        [whole] * 4,
        (square, whole, whole),
        band,
        row_count,
        flops,
    )
    later_codes = jnp.concatenate([*codes(c_far, c_last), grp_pos.reshape(1)])

    def later_loads(start):
        return [
            (0, 0, 0, 0, part, None),
            (1, start, 1, 0, part, None),
            (2, 0, 2, 0, part, None),
            (3, start, 3, 0, part, None),
            (4, 0, 4, 0, full, None),
            (5, 0, 5, 0, full, None),
            (6, 0, 6, 0, full, 0),
            (7, 0, 6, 0, full, 1),
        ]

    rights = (p_own, partner, beyond_even, beyond_odd)
    earlier = run_products(
        mid_kernel,
        later_codes,
        (a_far[0], p_far, a_last[0], p_last, *rights, partial, kept_1, kept_2),
        later_loads(0)
        + [
            (8, 0, 7, 0, width, None),
            (9, 0, 8, 0, full, None),
            (10, 0, 9, 0, full, None),
        ],
        [piece] * 4 + [whole] * 3 + [square, whole, whole],
        wide,
        band,
        row_count,
        flops,
    )
    keep, send = run_products(
        late_kernel,
        later_codes,
        (a_far[1], p_far, a_last[1], p_last, *rights, earlier),
        later_loads(part) + [(8, 0, 7, 0, width, None)],
        [piece] * 4 + [whole] * 3 + [wide],
        (half, half),
        band,
        row_count,
        flops,
    )
    share = width // groups
    pair = keep + xor_permute(send, "grp", 1)
    total = pair[:share] + xor_permute(pair[share:], "grp", 2)
    total = total.astype(jnp.bfloat16)
    own, direct, diagonal = (total[:, i * width : (i + 1) * width] for i in range(SLOTS))
    even = rows_pos % 2 == 0
    return jnp.concatenate(
        [jnp.where(even, diagonal, direct), own, jnp.where(even, direct, diagonal)], axis=1
    )


def pack_kernel(names, capacity, pieces, slot_ref, a_hbm, *refs):
    count = len(names)
    outs, (a_ref, packed, sems_in, sems_out) = refs[:count], refs[count:]
    columns = a_ref.shape[1] // pieces
    loads = [
        pltpu.make_async_copy(
            a_hbm.at[:, pl.ds(i * columns, columns)],
            a_ref.at[:, pl.ds(i * columns, columns)],
            sems_in.at[i],
        )
        for i in range(pieces)
    ]
    for copy in loads:
        copy.start()
    shape = (capacity, a_ref.shape[0])
    hot = jnp.concatenate(
        [
            (lax.broadcasted_iota(jnp.int32, shape, 0) + name * capacity == slot_ref[...]).astype(
                jnp.float32
            )
            for name in names
        ],
        axis=0,
    )
    empty = jnp.sum(hot, axis=1, keepdims=True) < 0.5
    hot = hot.astype(jnp.bfloat16)
    stores = []
    for i in range(pieces):
        loads[i].wait()
        at = slice(i * columns, (i + 1) * columns)
        packed[:, at] = jnp.dot(
            hot, a_ref[:, at], preferred_element_type=jnp.float32
        ).astype(jnp.bfloat16)
        if i == 0:
            first = packed[:, :128].astype(jnp.float32)
            packed[:, :128] = jnp.where(empty, jnp.inf, first).astype(jnp.bfloat16)
        for chunk in range(count):
            copy = pltpu.make_async_copy(
                packed.at[pl.ds(chunk * capacity, capacity), pl.ds(i * columns, columns)],
                outs[chunk].at[:, pl.ds(i * columns, columns)],
                sems_out.at[chunk * pieces + i],
            )
            copy.start()
            stores.append(copy)
    for copy in stores:
        copy.wait()


def pack_chunks(a_vals, slot_of, names, capacity):
    row_count, row_width = a_vals.shape
    pieces, count = 4, len(names)
    out = pl.pallas_call(
        functools.partial(pack_kernel, names, capacity, pieces),
        out_shape=[jax.ShapeDtypeStruct((capacity, row_width), a_vals.dtype)] * count,
        in_specs=[pl.BlockSpec(memory_space=pltpu.VMEM), pl.BlockSpec(memory_space=pl.ANY)],
        out_specs=[pl.BlockSpec(memory_space=pl.ANY)] * count,
        scratch_shapes=[
            pltpu.VMEM((row_count, row_width), a_vals.dtype),
            pltpu.VMEM((count * capacity, row_width), a_vals.dtype),
            pltpu.SemaphoreType.DMA((pieces,)),
            pltpu.SemaphoreType.DMA((count * pieces,)),
        ],
    )(slot_of[None, :], a_vals)
    return dict(zip(names, out))


def gather_kernel(chunks, capacity, where, *refs):
    sources, (target, probe, buffer, sems_probe, sems_in, sems_out) = refs[:chunks], refs[chunks:]
    probes = [
        pltpu.make_async_copy(
            sources[c].at[:, pl.ds(0, probe.shape[2])], probe.at[c], sems_probe.at[c]
        )
        for c in range(chunks)
    ]
    for copy in probes:
        copy.start()
    full = []
    for c in range(chunks):
        probes[c].wait()
        full.append(jnp.where(jnp.max(probe[c].astype(jnp.float32)) < jnp.inf, 1, 0))
    limit = target.shape[0] // capacity - 1
    place = []
    for c in range(chunks):
        sender = jnp.bitwise_xor(where[0], c)
        ahead = jnp.int32(0)
        for other in range(chunks):
            first = jnp.bitwise_xor(where[0], other) < sender
            ahead = ahead + jnp.where(first, full[other], 0)
        place.append(pl.multiple_of(jnp.minimum(ahead, limit) * capacity, capacity))

    def loads(c):
        return pltpu.make_async_copy(
            sources[c], buffer.at[pl.ds(place[c], capacity), :], sems_in.at[c]
        )

    def stores(c):
        return pltpu.make_async_copy(
            buffer.at[pl.ds(place[c], capacity), :],
            target.at[pl.ds(place[c], capacity), :],
            sems_out.at[c],
        )

    for c in range(chunks):
        pl.when(full[c] == 1)(lambda c=c: loads(c).start())
    for c in range(chunks):
        @pl.when(full[c] == 1)
        def _():
            loads(c).wait()
            stores(c).start()

    for c in range(chunks):
        pl.when(full[c] == 1)(lambda c=c: stores(c).wait())


def gather_chunks(incoming, rows_pos, row_count):
    chunks = len(incoming)
    capacity, row_width = incoming[0].shape
    dtype = incoming[0].dtype
    return pl.pallas_call(
        functools.partial(gather_kernel, chunks, capacity),
        out_shape=jax.ShapeDtypeStruct((row_count, row_width), dtype),
        in_specs=[pl.BlockSpec(memory_space=pltpu.SMEM)]
        + [pl.BlockSpec(memory_space=pl.ANY)] * chunks,
        out_specs=pl.BlockSpec(memory_space=pl.ANY),
        scratch_shapes=[
            pltpu.VMEM((chunks, capacity, 128), dtype),
            pltpu.VMEM((row_count, row_width), dtype),
            pltpu.SemaphoreType.DMA((chunks,)),
            pltpu.SemaphoreType.DMA((chunks,)),
            pltpu.SemaphoreType.DMA((chunks,)),
        ],
        name="gather_chunks",
    )(rows_pos.astype(jnp.int32).reshape(1), *incoming)


def use_chunks(row_count, rows_total):
    capacity = max(2, 2 * row_count // rows_total)
    return capacity % 16 == 0 and rows_total & (rows_total - 1) == 0


def migrate(a_vals, new_rows):
    row_count, row_width = a_vals.shape
    rows_total = lax.axis_size("rows")
    capacity = max(2, 2 * row_count // rows_total)
    slot_total = rows_total * capacity
    earlier = jnp.arange(row_count)[None, :] < jnp.arange(row_count)[:, None]
    same = new_rows[:, None] == new_rows[None, :]
    ranking = jnp.sum((earlier & same).astype(jnp.int32), axis=1)
    if use_chunks(row_count, rows_total):
        rows_pos = lax.axis_index("rows")
        slot_of = jnp.bitwise_xor(new_rows, rows_pos) * capacity + ranking
        first = tuple(range(rows_total // 2, rows_total, 2))
        rest = tuple(i for i in range(rows_total) if i not in first)
        chunks = pack_chunks(a_vals, slot_of, first, capacity)
        chunks |= pack_chunks(a_vals, slot_of, rest, capacity)
        incoming = [chunks[0]] + [
            xor_permute(chunks[bit], "rows", bit)
            for bit in range(1, rows_total)
        ]
        return gather_chunks(incoming, rows_pos, row_count)
    slot_of = new_rows * capacity + ranking
    slot_ids = jnp.arange(slot_total, dtype=jnp.int32)
    sender = slot_ids[:, None] == slot_of[None, :]
    picked = jnp.dot(sender.astype(jnp.bfloat16), a_vals, preferred_element_type=jnp.float32)
    filled = jnp.any(sender, axis=1)
    incoming = lax.all_to_all(
        picked.astype(a_vals.dtype).reshape(rows_total, capacity, row_width),
        "rows",
        split_axis=0,
        concat_axis=0,
        tiled=True,
    ).reshape(slot_total, row_width)
    flags = lax.all_to_all(
        filled.astype(jnp.bfloat16).reshape(rows_total, capacity),
        "rows",
        split_axis=0,
        concat_axis=0,
        tiled=True,
    )
    flat_flags = flags.reshape(slot_total).astype(jnp.float32)
    position = jnp.cumsum(flat_flags) - 1.0
    wanted = jnp.arange(row_count, dtype=jnp.float32)
    receiver = (position[None, :] == wanted[:, None]) & (flat_flags[None, :] > 0.0)
    return jnp.dot(
        receiver.astype(jnp.bfloat16), incoming, preferred_element_type=jnp.float32
    ).astype(a_vals.dtype)


def local(a_vals, a_cols, p_vals, new_rows):
    a_moved = migrate(a_vals, new_rows)
    coarse = galerkin(a_vals, a_cols, p_vals)
    return (a_moved, coarse)


def solution(mesh):
    in_specs = (
        P(("rows", "grp"), None),
        P(("rows", "grp"), None),
        P(("rows", "grp"), None),
        P(("rows", "grp")),
    )
    out_specs = (P(("rows", "grp"), None), P(("rows", "grp"), None))
    return jax.shard_map(local, mesh=mesh, in_specs=in_specs, out_specs=out_specs, check_vma=False)
```

```python
import functools

import jax
import jax.numpy as jnp
from jax import lax
from jax.experimental import pallas as pl
from jax.experimental.pallas import tpu as pltpu
from jax.sharding import PartitionSpec as P


B = 64
UNROLL = 8
SLOTS = 3


def xor_permute(value, axis, bit):
    count = lax.axis_size(axis)
    return lax.ppermute(value, axis, [(i, i ^ bit) for i in range(count)])


def entry_codes(cols, rows_pos, grp_pos, groups):
    row_count, band = cols.shape
    device = cols // row_count
    near = device // groups - rows_pos
    side = jnp.where(rows_pos % 2 == 1, -near, near)
    slot = jnp.where(near == 0, 0, jnp.where(side == 1, 1, 2))
    target = slot * row_count + cols % row_count
    entry = jnp.arange(row_count, dtype=jnp.int32)[:, None] * band + jnp.arange(
        band, dtype=jnp.int32
    )
    code = entry * target_span(row_count) + target
    return jnp.where(device % groups == grp_pos, code, -1).reshape(-1)


def target_span(row_count):
    return pl.next_power_of_2(SLOTS * row_count + 1)


def clear(sums):
    rows = 2 * B

    def step(i, _):
        sums[pl.ds(pl.multiple_of(i * rows, rows), rows), :] = jnp.zeros(
            (rows, sums.shape[1]), sums.dtype
        )
        return 0

    lax.fori_loop(0, sums.shape[0] // rows, step, 0)


def scatter_part(band, row_count, offset, base, code_ref, a_ref, p_ref, sums, order):
    entries = a_ref.shape[0] // B * band
    span = target_span(row_count)
    dummy = base * band * span + SLOTS * row_count

    def collect(step, found):
        code = code_ref[offset + base * band + step]
        order[found] = code
        return found + jnp.where(code >= 0, 1, 0)

    count = lax.fori_loop(0, entries, collect, 0, unroll=16)
    for pad in range(UNROLL):
        order[count + pad] = dummy

    def batch(step, _):
        terms = []
        for lane in range(UNROLL):
            code = order[step * UNROLL + lane]
            target = jnp.bitwise_and(code, span - 1)
            entry = lax.div(code, span)
            row = lax.div(entry, band) - base
            k = lax.rem(entry, band)
            start = pl.multiple_of(row * B, B)
            half = pl.multiple_of(lax.div(k, 2) * (2 * B), 2 * B)
            block = a_ref[pl.ds(start, B), pl.ds(half, 2 * B)]
            block = jnp.where(lax.rem(k, 2) == 1, block[:, B:], block[:, :B])
            left = p_ref[pl.ds(start, B), :]
            terms.append((contract(block, left), target))
        for term, target in terms:
            at = pl.ds(pl.multiple_of(target * B, B), B)
            sums[at, :] = sums[at, :] + term
        return 0

    lax.fori_loop(0, lax.div(count + UNROLL - 1, UNROLL), batch, 0)


def contract(left, right):
    return lax.dot_general(
        left, right, (((0,), (0,)), ((), ())), preferred_element_type=jnp.float32
    )


def copies_of(loads, sources, buffers, sems, parity):
    copies = []
    for i, (source, start, buffer, at, rows, when) in enumerate(loads):
        copy = pltpu.make_async_copy(
            sources[source].at[pl.ds(start, rows), :],
            buffers[buffer].at[pl.ds(at, rows), :],
            sems.at[i],
        )
        copies.append((copy, when))
        if when is None:
            copy.start()
        else:
            pl.when(parity == when)(copy.start)

    def wait(i):
        copy, when = copies[i]
        if when is None:
            copy.wait()
        else:
            pl.when(parity == when)(copy.wait)

    return wait


def early_kernel(band, row_count, loads, inputs, codes, *refs):
    sources, (partial, kept_1, kept_2), refs = refs[:inputs], refs[inputs : inputs + 3], refs[inputs + 3 :]
    buffers, (sums, order, sems) = refs[:-3], refs[-3:]
    wait = copies_of(loads, sources, buffers, sems, None)
    clear(sums)
    for part in range(2):
        for i in range(3):
            wait(3 * part + i)
        a_ref, p_ref = buffers[2 * part : 2 * part + 2]
        scatter_part(
            band, row_count, part * row_count * band, 0, codes, a_ref, p_ref, sums, order
        )
    size = row_count * B
    partial[...] = contract(sums[:size].astype(jnp.bfloat16), buffers[1][...])
    kept_1[...] = sums[size : 2 * size].astype(jnp.bfloat16)
    kept_2[...] = sums[2 * size : 3 * size].astype(jnp.bfloat16)


def later_sums(band, row_count, base, wait, codes, buffers, sums, order):
    clear(sums)
    for part in range(2):
        wait(2 * part)
        wait(2 * part + 1)
        a_ref, p_ref = buffers[2 * part : 2 * part + 2]
        scatter_part(
            band, row_count, part * row_count * band, base, codes, a_ref, p_ref, sums, order
        )


def mid_kernel(band, row_count, loads, inputs, codes, *refs):
    sources, result, refs = refs[:inputs], refs[inputs], refs[inputs + 1 :]
    buffers, (sums, order, sems) = refs[:-3], refs[-3:]
    parity = lax.rem(codes[2 * row_count * band], 2)
    wait = copies_of(loads, sources, buffers, sems, parity)
    later_sums(band, row_count, 0, wait, codes, buffers, sums, order)
    for i in range(4, len(loads)):
        wait(i)
    size = row_count * B
    rights, partial, kept = buffers[4 : 4 + SLOTS], buffers[4 + SLOTS], buffers[5 + SLOTS :]
    width = partial.shape[1]
    for slot in range(SLOTS):
        right = rights[slot][...]
        here = contract(sums[slot * size : (slot + 1) * size].astype(jnp.bfloat16), right)
        if slot == 0:
            here = here + partial[...]
        else:
            here = here + contract(kept[slot - 1][...], right)
        result[:, slot * width : (slot + 1) * width] = here


def late_kernel(band, row_count, loads, inputs, codes, *refs):
    sources, (keep, send), refs = refs[:inputs], refs[inputs : inputs + 2], refs[inputs + 2 :]
    buffers, (sums, order, sems) = refs[:-3], refs[-3:]
    grp_pos = codes[2 * row_count * band]
    wait = copies_of(loads, sources, buffers, sems, lax.rem(grp_pos, 2))
    later_sums(band, row_count, row_count // 2, wait, codes, buffers, sums, order)
    for i in range(4, len(loads)):
        wait(i)
    size = row_count * B
    rights, earlier = buffers[4 : 4 + SLOTS], buffers[4 + SLOTS]
    width = rights[0].shape[1]
    share = keep.shape[0] // 2
    for slot in range(SLOTS):
        columns = slice(slot * width, (slot + 1) * width)
        here = contract(
            sums[slot * size : (slot + 1) * size].astype(jnp.bfloat16), rights[slot][...]
        )
        here = here + earlier[:, columns]
        for block in range(width // share):
            piece = here[block * share : (block + 1) * share]
            place = jnp.bitwise_xor(block, grp_pos)
            at = pl.ds(pl.multiple_of(lax.div(place, 2) * share, share), share)

            @pl.when(lax.rem(place, 2) == 0)
            def _():
                keep[at, columns] = piece

            @pl.when(lax.rem(place, 2) == 1)
            def _():
                send[at, columns] = piece


def run_products(body, codes, arrays, loads, buffers, outs, band, row_count, flops):
    width = arrays[0].shape[1]
    held = sum(x.size * x.dtype.itemsize for x in buffers) + SLOTS * row_count * B * width * 4
    return pl.pallas_call(
        functools.partial(body, band, row_count, loads, len(arrays)),
        out_shape=outs,
        in_specs=[pl.BlockSpec(memory_space=pltpu.SMEM)]
        + [pl.BlockSpec(memory_space=pl.ANY)] * len(arrays),
        out_specs=jax.tree.map(lambda _: pl.BlockSpec(memory_space=pltpu.VMEM), outs),
        scratch_shapes=[pltpu.VMEM(x.shape, x.dtype) for x in buffers]
        + [
            pltpu.VMEM(((SLOTS * row_count + 2) * B, width), jnp.float32),
            pltpu.SMEM((row_count * band + UNROLL,), jnp.int32),
            pltpu.SemaphoreType.DMA((len(loads),)),
        ],
        compiler_params=pltpu.CompilerParams(vmem_limit_bytes=held + (16 << 20)),
        cost_estimate=pl.CostEstimate(
            flops=flops,
            bytes_accessed=sum(x.size * x.dtype.itemsize for x in arrays),
            transcendentals=0,
        ),
    )(codes, *arrays)


def galerkin(a_vals, a_cols, p_vals):
    row_count, band = a_cols.shape
    width = p_vals.shape[1] // B
    rows_total, groups = lax.axis_size("rows"), lax.axis_size("grp")
    rows_pos, grp_pos = lax.axis_index("rows"), lax.axis_index("grp")
    assert groups == 4 and rows_total % 2 == 0
    p_own = p_vals.reshape(row_count * B, width)
    cut = row_count // 2
    a_own = [a_vals[i * cut : (i + 1) * cut].reshape(cut * B, band * B) for i in range(2)]

    partner = xor_permute(p_own, "rows", 1)
    both = ("rows", "grp")
    ahead = [
        (i * groups + g, j * groups + g)
        for g in range(1, groups, 2)
        for i in range(rows_total)
        for j in [i + 2 if i % 2 else i - 2]
        if 0 <= j < rows_total
    ]
    onward = [
        (i * groups + g, j * groups + g)
        for g in range(0, groups, 2)
        for i in range(rows_total)
        for j in [i - 2 if i % 2 else i + 2]
        if 0 <= j < rows_total
    ]
    across = [
        (i * groups + g, (i ^ 1) * groups + g)
        for g in range(1, groups, 2)
        for i in range(rows_total)
    ]
    moved = lax.ppermute(p_own, both, ahead)
    beyond_even = lax.ppermute(partner, both, onward)
    beyond_odd = lax.ppermute(moved, both, across)

    c_far = xor_permute(a_cols, "grp", 2)
    c_near = xor_permute(a_cols, "grp", 1)
    c_last = xor_permute(c_far, "grp", 1)
    p_far = xor_permute(p_own, "grp", 2)
    p_near = xor_permute(p_own, "grp", 1)
    p_last = xor_permute(p_far, "grp", 1)
    a_far = [xor_permute(a_own[i], "grp", 2) for i in range(2)]
    a_near = [xor_permute(a_own[i], "grp", 1) for i in range(2)]
    a_last = [xor_permute(a_far[i], "grp", 1) for i in range(2)]

    def codes(*cols):
        return [entry_codes(c, rows_pos, grp_pos, groups) for c in cols]

    flops = 4 * row_count * band * B * B * width // 2
    full, part = row_count * B, cut * B
    whole = jax.ShapeDtypeStruct((full, width), jnp.bfloat16)
    piece = jax.ShapeDtypeStruct((part, width), jnp.bfloat16)
    square = jax.ShapeDtypeStruct((width, width), jnp.float32)
    wide = jax.ShapeDtypeStruct((width, SLOTS * width), jnp.float32)
    half = jax.ShapeDtypeStruct((width // 2, SLOTS * width), jnp.float32)
    partial, kept_1, kept_2 = run_products(
        early_kernel,
        jnp.concatenate(codes(a_cols, c_near)),
        (*a_own, p_own, *a_near, p_near),
        [
            (0, 0, 0, 0, part, None),
            (1, 0, 0, part, part, None),
            (2, 0, 1, 0, full, None),
            (3, 0, 2, 0, part, None),
            (4, 0, 2, part, part, None),
            (5, 0, 3, 0, full, None),
        ],
        [whole] * 4,
        (square, whole, whole),
        band,
        row_count,
        flops,
    )
    later_codes = jnp.concatenate([*codes(c_far, c_last), grp_pos.reshape(1)])

    def later_loads(start):
        return [
            (0, 0, 0, 0, part, None),
            (1, start, 1, 0, part, None),
            (2, 0, 2, 0, part, None),
            (3, start, 3, 0, part, None),
            (4, 0, 4, 0, full, None),
            (5, 0, 5, 0, full, None),
            (6, 0, 6, 0, full, 0),
            (7, 0, 6, 0, full, 1),
        ]

    rights = (p_own, partner, beyond_even, beyond_odd)
    earlier = run_products(
        mid_kernel,
        later_codes,
        (a_far[0], p_far, a_last[0], p_last, *rights, partial, kept_1, kept_2),
        later_loads(0)
        + [
            (8, 0, 7, 0, width, None),
            (9, 0, 8, 0, full, None),
            (10, 0, 9, 0, full, None),
        ],
        [piece] * 4 + [whole] * 3 + [square, whole, whole],
        wide,
        band,
        row_count,
        flops,
    )
    keep, send = run_products(
        late_kernel,
        later_codes,
        (a_far[1], p_far, a_last[1], p_last, *rights, earlier),
        later_loads(part) + [(8, 0, 7, 0, width, None)],
        [piece] * 4 + [whole] * 3 + [wide],
        (half, half),
        band,
        row_count,
        flops,
    )
    share = width // groups
    pair = keep + xor_permute(send, "grp", 1)
    total = pair[:share] + xor_permute(pair[share:], "grp", 2)
    total = total.astype(jnp.bfloat16)
    own, direct, diagonal = (total[:, i * width : (i + 1) * width] for i in range(SLOTS))
    even = rows_pos % 2 == 0
    return jnp.concatenate(
        [jnp.where(even, diagonal, direct), own, jnp.where(even, direct, diagonal)], axis=1
    )


def pack_kernel(names, capacity, pieces, slot_ref, a_hbm, *refs):
    count = len(names)
    outs, (a_ref, packed, sems_in, sems_out) = refs[:count], refs[count:]
    columns = a_ref.shape[1] // pieces
    loads = [
        pltpu.make_async_copy(
            a_hbm.at[:, pl.ds(i * columns, columns)],
            a_ref.at[:, pl.ds(i * columns, columns)],
            sems_in.at[i],
        )
        for i in range(pieces)
    ]
    for copy in loads:
        copy.start()
    shape = (capacity, a_ref.shape[0])
    hot = jnp.concatenate(
        [
            (lax.broadcasted_iota(jnp.int32, shape, 0) + name * capacity == slot_ref[...]).astype(
                jnp.float32
            )
            for name in names
        ],
        axis=0,
    )
    empty = jnp.sum(hot, axis=1, keepdims=True) < 0.5
    hot = hot.astype(jnp.bfloat16)
    stores = []
    for i in range(pieces):
        loads[i].wait()
        at = slice(i * columns, (i + 1) * columns)
        packed[:, at] = jnp.dot(
            hot, a_ref[:, at], preferred_element_type=jnp.float32
        ).astype(jnp.bfloat16)
        if i == 0:
            first = packed[:, :128].astype(jnp.float32)
            packed[:, :128] = jnp.where(empty, jnp.inf, first).astype(jnp.bfloat16)
        for chunk in range(count):
            copy = pltpu.make_async_copy(
                packed.at[pl.ds(chunk * capacity, capacity), pl.ds(i * columns, columns)],
                outs[chunk].at[:, pl.ds(i * columns, columns)],
                sems_out.at[chunk * pieces + i],
            )
            copy.start()
            stores.append(copy)
    for copy in stores:
        copy.wait()


def pack_chunks(a_vals, slot_of, names, capacity):
    row_count, row_width = a_vals.shape
    pieces, count = 4, len(names)
    out = pl.pallas_call(
        functools.partial(pack_kernel, names, capacity, pieces),
        out_shape=[jax.ShapeDtypeStruct((capacity, row_width), a_vals.dtype)] * count,
        in_specs=[pl.BlockSpec(memory_space=pltpu.VMEM), pl.BlockSpec(memory_space=pl.ANY)],
        out_specs=[pl.BlockSpec(memory_space=pl.ANY)] * count,
        scratch_shapes=[
            pltpu.VMEM((row_count, row_width), a_vals.dtype),
            pltpu.VMEM((count * capacity, row_width), a_vals.dtype),
            pltpu.SemaphoreType.DMA((pieces,)),
            pltpu.SemaphoreType.DMA((count * pieces,)),
        ],
    )(slot_of[None, :], a_vals)
    return dict(zip(names, out))


def toward(position, bit):
    return (position % 2 == 0) == ((position ^ bit) > position)


def gather_kernel(names, split, capacity, where, *refs):
    chunks, total = len(names), len(names) + len(split)
    sources, (target, probe, buffer, sems_probe, sems_in, sems_out) = refs[:total], refs[total:]
    me = where[0]
    even = jnp.where(lax.rem(me, 2) == 0, 1, 0)

    def each(c, make, act):
        if names[c] not in split:
            act(make(sources[c]))
            return
        above = jnp.where(me > jnp.bitwise_xor(me, names[c]), 1, 0)
        other = sources[chunks + split.index(names[c])]
        pl.when(even == above)(lambda: act(make(sources[c])))
        pl.when(even != above)(lambda: act(make(other)))

    def probes(c):
        return lambda source: pltpu.make_async_copy(
            source.at[:, pl.ds(0, probe.shape[2])], probe.at[c], sems_probe.at[c]
        )

    for c in range(chunks):
        each(c, probes(c), lambda copy: copy.start())
    full = []
    for c in range(chunks):
        each(c, probes(c), lambda copy: copy.wait())
        full.append(jnp.where(jnp.max(probe[c].astype(jnp.float32)) < jnp.inf, 1, 0))
    limit = target.shape[0] // capacity - 1
    place = []
    for c in range(chunks):
        sender = jnp.bitwise_xor(me, names[c])
        ahead = jnp.int32(0)
        for other in range(chunks):
            first = jnp.bitwise_xor(me, names[other]) < sender
            ahead = ahead + jnp.where(first, full[other], 0)
        place.append(pl.multiple_of(jnp.minimum(ahead, limit) * capacity, capacity))

    def loads(c):
        return lambda source: pltpu.make_async_copy(
            source, buffer.at[pl.ds(place[c], capacity), :], sems_in.at[c]
        )

    def stores(c):
        return pltpu.make_async_copy(
            buffer.at[pl.ds(place[c], capacity), :],
            target.at[pl.ds(place[c], capacity), :],
            sems_out.at[c],
        )

    for c in range(chunks):
        @pl.when(full[c] == 1)
        def _():
            each(c, loads(c), lambda copy: copy.start())

    for c in range(chunks):
        @pl.when(full[c] == 1)
        def _():
            each(c, loads(c), lambda copy: copy.wait())
            stores(c).start()

    for c in range(chunks):
        pl.when(full[c] == 1)(lambda c=c: stores(c).wait())


def gather_chunks(incoming, others, rows_pos, row_count):
    names, split = tuple(incoming), tuple(others)
    chunks = len(names)
    capacity, row_width = incoming[0].shape
    dtype = incoming[0].dtype
    return pl.pallas_call(
        functools.partial(gather_kernel, names, split, capacity),
        out_shape=jax.ShapeDtypeStruct((row_count, row_width), dtype),
        in_specs=[pl.BlockSpec(memory_space=pltpu.SMEM)]
        + [pl.BlockSpec(memory_space=pl.ANY)] * (chunks + len(split)),
        out_specs=pl.BlockSpec(memory_space=pl.ANY),
        scratch_shapes=[
            pltpu.VMEM((chunks, capacity, 128), dtype),
            pltpu.VMEM((row_count, row_width), dtype),
            pltpu.SemaphoreType.DMA((chunks,)),
            pltpu.SemaphoreType.DMA((chunks,)),
            pltpu.SemaphoreType.DMA((chunks,)),
        ],
        name="gather_chunks",
    )(rows_pos.astype(jnp.int32).reshape(1), *incoming.values(), *others.values())


def use_chunks(row_count, rows_total):
    capacity = max(2, 2 * row_count // rows_total)
    return capacity % 16 == 0 and rows_total & (rows_total - 1) == 0


def migrate(a_vals, new_rows):
    row_count, row_width = a_vals.shape
    rows_total = lax.axis_size("rows")
    capacity = max(2, 2 * row_count // rows_total)
    slot_total = rows_total * capacity
    earlier = jnp.arange(row_count)[None, :] < jnp.arange(row_count)[:, None]
    same = new_rows[:, None] == new_rows[None, :]
    ranking = jnp.sum((earlier & same).astype(jnp.int32), axis=1)
    if use_chunks(row_count, rows_total):
        rows_pos = lax.axis_index("rows")
        slot_of = jnp.bitwise_xor(new_rows, rows_pos) * capacity + ranking
        first = tuple(range(rows_total // 2, rows_total, 2))
        rest = tuple(i for i in range(rows_total) if i not in first)
        chunks = pack_chunks(a_vals, slot_of, first, capacity)
        chunks |= pack_chunks(a_vals, slot_of, rest, capacity)
        incoming, others = {0: chunks[0]}, {}
        for bit in range(1, rows_total):
            pairs = [(i, i ^ bit) for i in range(rows_total)]
            if bit in first:
                back = [pair for pair in pairs if not toward(pair[0], bit)]
                pairs = [pair for pair in pairs if toward(pair[0], bit)]
                others[bit] = lax.ppermute(chunks[bit], "rows", back)
            incoming[bit] = lax.ppermute(chunks[bit], "rows", pairs)
        return gather_chunks(incoming, others, rows_pos, row_count)
    slot_of = new_rows * capacity + ranking
    slot_ids = jnp.arange(slot_total, dtype=jnp.int32)
    sender = slot_ids[:, None] == slot_of[None, :]
    picked = jnp.dot(sender.astype(jnp.bfloat16), a_vals, preferred_element_type=jnp.float32)
    filled = jnp.any(sender, axis=1)
    incoming = lax.all_to_all(
        picked.astype(a_vals.dtype).reshape(rows_total, capacity, row_width),
        "rows",
        split_axis=0,
        concat_axis=0,
        tiled=True,
    ).reshape(slot_total, row_width)
    flags = lax.all_to_all(
        filled.astype(jnp.bfloat16).reshape(rows_total, capacity),
        "rows",
        split_axis=0,
        concat_axis=0,
        tiled=True,
    )
    flat_flags = flags.reshape(slot_total).astype(jnp.float32)
    position = jnp.cumsum(flat_flags) - 1.0
    wanted = jnp.arange(row_count, dtype=jnp.float32)
    receiver = (position[None, :] == wanted[:, None]) & (flat_flags[None, :] > 0.0)
    return jnp.dot(
        receiver.astype(jnp.bfloat16), incoming, preferred_element_type=jnp.float32
    ).astype(a_vals.dtype)


def local(a_vals, a_cols, p_vals, new_rows):
    a_moved = migrate(a_vals, new_rows)
    coarse = galerkin(a_vals, a_cols, p_vals)
    return (a_moved, coarse)


def solution(mesh):
    in_specs = (
        P(("rows", "grp"), None),
        P(("rows", "grp"), None),
        P(("rows", "grp"), None),
        P(("rows", "grp")),
    )
    out_specs = (P(("rows", "grp"), None), P(("rows", "grp"), None))
    return jax.shard_map(local, mesh=mesh, in_specs=in_specs, out_specs=out_specs, check_vma=False)
```

```python
import functools

import jax
import jax.numpy as jnp
from jax import lax
from jax.experimental import pallas as pl
from jax.experimental.pallas import tpu as pltpu
from jax.sharding import PartitionSpec as P


B = 64
UNROLL = 8
SLOTS = 3


def xor_permute(value, axis, bit):
    count = lax.axis_size(axis)
    return lax.ppermute(value, axis, [(i, i ^ bit) for i in range(count)])


def entry_codes(cols, rows_pos, grp_pos, groups):
    row_count, band = cols.shape
    device = cols // row_count
    near = device // groups - rows_pos
    side = jnp.where(rows_pos % 2 == 1, -near, near)
    slot = jnp.where(near == 0, 0, jnp.where(side == 1, 1, 2))
    target = slot * row_count + cols % row_count
    entry = jnp.arange(row_count, dtype=jnp.int32)[:, None] * band + jnp.arange(
        band, dtype=jnp.int32
    )
    code = entry * target_span(row_count) + target
    return jnp.where(device % groups == grp_pos, code, -1).reshape(-1)


def target_span(row_count):
    return pl.next_power_of_2(SLOTS * row_count + 1)


def clear(sums):
    rows = 2 * B

    def step(i, _):
        sums[pl.ds(pl.multiple_of(i * rows, rows), rows), :] = jnp.zeros(
            (rows, sums.shape[1]), sums.dtype
        )
        return 0

    lax.fori_loop(0, sums.shape[0] // rows, step, 0)


def scatter_part(band, row_count, offset, base, code_ref, a_ref, p_ref, sums, order):
    entries = a_ref.shape[0] // B * band
    span = target_span(row_count)
    dummy = base * band * span + SLOTS * row_count

    def collect(step, found):
        code = code_ref[offset + base * band + step]
        order[found] = code
        return found + jnp.where(code >= 0, 1, 0)

    count = lax.fori_loop(0, entries, collect, 0, unroll=16)
    for pad in range(UNROLL):
        order[count + pad] = dummy

    def batch(step, _):
        terms = []
        for lane in range(UNROLL):
            code = order[step * UNROLL + lane]
            target = jnp.bitwise_and(code, span - 1)
            entry = lax.div(code, span)
            row = lax.div(entry, band) - base
            k = lax.rem(entry, band)
            start = pl.multiple_of(row * B, B)
            half = pl.multiple_of(lax.div(k, 2) * (2 * B), 2 * B)
            block = a_ref[pl.ds(start, B), pl.ds(half, 2 * B)]
            block = jnp.where(lax.rem(k, 2) == 1, block[:, B:], block[:, :B])
            left = p_ref[pl.ds(start, B), :]
            terms.append((contract(block, left), target))
        for term, target in terms:
            at = pl.ds(pl.multiple_of(target * B, B), B)
            sums[at, :] = sums[at, :] + term
        return 0

    lax.fori_loop(0, lax.div(count + UNROLL - 1, UNROLL), batch, 0)


def contract(left, right):
    return lax.dot_general(
        left, right, (((0,), (0,)), ((), ())), preferred_element_type=jnp.float32
    )


def copies_of(loads, sources, buffers, sems):
    copies = []
    for i, (source, start, buffer, at, rows) in enumerate(loads):
        copy = pltpu.make_async_copy(
            sources[source].at[pl.ds(start, rows), :],
            buffers[buffer].at[pl.ds(at, rows), :],
            sems.at[i],
        )
        copies.append(copy)
        copy.start()
    return lambda i: copies[i].wait()


def early_kernel(band, row_count, loads, inputs, codes, *refs):
    sources, (partial, kept_1, kept_2), refs = refs[:inputs], refs[inputs : inputs + 3], refs[inputs + 3 :]
    buffers, (sums, order, sems) = refs[:-3], refs[-3:]
    wait = copies_of(loads, sources, buffers, sems)
    clear(sums)
    for part in range(2):
        for i in range(3):
            wait(3 * part + i)
        a_ref, p_ref = buffers[2 * part : 2 * part + 2]
        scatter_part(
            band, row_count, part * row_count * band, 0, codes, a_ref, p_ref, sums, order
        )
    size = row_count * B
    stores = []
    for slot, kept in ((1, kept_1), (2, kept_2)):
        staged = buffers[2 * (slot - 1)]
        staged[...] = sums[slot * size : (slot + 1) * size].astype(jnp.bfloat16)
        stores.append(pltpu.make_async_copy(staged, kept, sems.at[len(loads) + slot - 1]))
        stores[-1].start()
    partial[...] = contract(sums[:size].astype(jnp.bfloat16), buffers[1][...])
    for copy in stores:
        copy.wait()


def later_sums(band, row_count, base, wait, codes, buffers, sums, order):
    clear(sums)
    for part in range(2):
        wait(2 * part)
        wait(2 * part + 1)
        a_ref, p_ref = buffers[2 * part : 2 * part + 2]
        scatter_part(
            band, row_count, part * row_count * band, base, codes, a_ref, p_ref, sums, order
        )


def mid_kernel(band, row_count, loads, inputs, codes, *refs):
    sources, result, refs = refs[:inputs], refs[inputs], refs[inputs + 1 :]
    buffers, (sums, order, sems) = refs[:-3], refs[-3:]
    wait = copies_of(loads, sources, buffers, sems)
    later_sums(band, row_count, 0, wait, codes, buffers, sums, order)
    for i in range(4, len(loads)):
        wait(i)
    size = row_count * B
    rights, partial, kept = buffers[4 : 4 + SLOTS], buffers[4 + SLOTS], buffers[5 + SLOTS :]
    width = partial.shape[1]
    for slot in range(SLOTS):
        right = rights[slot][...]
        here = contract(sums[slot * size : (slot + 1) * size].astype(jnp.bfloat16), right)
        if slot == 0:
            here = here + partial[...]
        else:
            here = here + contract(kept[slot - 1][...], right)
        result[:, slot * width : (slot + 1) * width] = here


def late_kernel(band, row_count, loads, inputs, codes, *refs):
    sources, (keep, send), refs = refs[:inputs], refs[inputs : inputs + 2], refs[inputs + 2 :]
    buffers, (sums, order, sems) = refs[:-3], refs[-3:]
    grp_pos = codes[2 * row_count * band]
    wait = copies_of(loads, sources, buffers, sems)
    later_sums(band, row_count, row_count // 2, wait, codes, buffers, sums, order)
    for i in range(4, len(loads)):
        wait(i)
    size = row_count * B
    rights, earlier = buffers[4 : 4 + SLOTS], buffers[4 + SLOTS]
    width = rights[0].shape[1]
    share = keep.shape[0] // 2
    for slot in range(SLOTS):
        columns = slice(slot * width, (slot + 1) * width)
        here = contract(
            sums[slot * size : (slot + 1) * size].astype(jnp.bfloat16), rights[slot][...]
        )
        here = here + earlier[:, columns]
        for block in range(width // share):
            piece = here[block * share : (block + 1) * share]
            place = jnp.bitwise_xor(block, grp_pos)
            at = pl.ds(pl.multiple_of(lax.div(place, 2) * share, share), share)

            @pl.when(lax.rem(place, 2) == 0)
            def _():
                keep[at, columns] = piece

            @pl.when(lax.rem(place, 2) == 1)
            def _():
                send[at, columns] = piece


def run_products(body, codes, arrays, loads, buffers, outs, band, row_count, flops, out_specs=None):
    width = arrays[0].shape[1]
    return pl.pallas_call(
        functools.partial(body, band, row_count, loads, len(arrays)),
        out_shape=outs,
        in_specs=[pl.BlockSpec(memory_space=pltpu.SMEM)]
        + [pl.BlockSpec(memory_space=pltpu.HBM)] * len(arrays),
        out_specs=out_specs
        or jax.tree.map(lambda _: pl.BlockSpec(memory_space=pltpu.VMEM), outs),
        scratch_shapes=[pltpu.VMEM(x.shape, x.dtype) for x in buffers]
        + [
            pltpu.VMEM(((SLOTS * row_count + 2) * B, width), jnp.float32),
            pltpu.SMEM((row_count * band + UNROLL,), jnp.int32),
            pltpu.SemaphoreType.DMA((len(loads) + 2,)),
        ],
        compiler_params=pltpu.CompilerParams(vmem_limit_bytes=60 << 20),
        cost_estimate=pl.CostEstimate(
            flops=flops,
            bytes_accessed=sum(x.size * x.dtype.itemsize for x in arrays),
            transcendentals=0,
        ),
    )(codes, *arrays)


def galerkin(a_vals, a_cols, p_vals):
    row_count, band = a_cols.shape
    width = p_vals.shape[1] // B
    rows_total, groups = lax.axis_size("rows"), lax.axis_size("grp")
    rows_pos, grp_pos = lax.axis_index("rows"), lax.axis_index("grp")
    assert groups == 4 and rows_total % 2 == 0
    p_own = p_vals.reshape(row_count * B, width)
    cut = row_count // 2
    a_own = [a_vals[i * cut : (i + 1) * cut].reshape(cut * B, band * B) for i in range(2)]

    cut = row_count // 2
    p_own = lax.optimization_barrier(p_own)
    p_half = [p_own[i * cut * B : (i + 1) * cut * B] for i in range(2)]
    partner = [xor_permute(p_half[i], "rows", 1) for i in range(2)]
    onward = [(i, j) for i in range(rows_total) for j in [i - 2 if i % 2 else i + 2]]
    ahead = [(i, j) for i in range(rows_total) for j in [i + 2 if i % 2 else i - 2]]
    onward, ahead = ([p for p in pairs if 0 <= p[1] < rows_total] for pairs in (onward, ahead))
    moved = lax.ppermute(p_half[1], "rows", ahead)
    beyond = [lax.ppermute(partner[0], "rows", onward), xor_permute(moved, "rows", 1)]

    c_far = xor_permute(a_cols, "grp", 2)
    c_near = xor_permute(a_cols, "grp", 1)
    c_last = xor_permute(c_far, "grp", 1)
    p_far = xor_permute(p_own, "grp", 2)
    p_near = xor_permute(p_own, "grp", 1)
    p_last = xor_permute(p_far, "grp", 1)
    a_far = [xor_permute(a_own[i], "grp", 2) for i in range(2)]
    a_near = [xor_permute(a_own[i], "grp", 1) for i in range(2)]
    a_last = [xor_permute(a_far[i], "grp", 1) for i in range(2)]

    def codes(*cols):
        return [entry_codes(c, rows_pos, grp_pos, groups) for c in cols]

    flops = 4 * row_count * band * B * B * width // 2
    full, part = row_count * B, cut * B
    whole = jax.ShapeDtypeStruct((full, width), jnp.bfloat16)
    piece = jax.ShapeDtypeStruct((part, width), jnp.bfloat16)
    square = jax.ShapeDtypeStruct((width, width), jnp.float32)
    wide = jax.ShapeDtypeStruct((width, SLOTS * width), jnp.float32)
    half = jax.ShapeDtypeStruct((width // 2, SLOTS * width), jnp.float32)
    partial, kept_1, kept_2 = run_products(
        early_kernel,
        jnp.concatenate(codes(a_cols, c_near)),
        (*a_own, p_own, *a_near, p_near),
        [
            (0, 0, 0, 0, part),
            (1, 0, 0, part, part),
            (2, 0, 1, 0, full),
            (3, 0, 2, 0, part),
            (4, 0, 2, part, part),
            (5, 0, 3, 0, full),
        ],
        [whole] * 4,
        (square, whole, whole),
        band,
        row_count,
        flops,
        (pl.BlockSpec(memory_space=pltpu.VMEM),) + (pl.BlockSpec(memory_space=pltpu.HBM),) * 2,
    )
    later_codes = jnp.concatenate([*codes(c_far, c_last), grp_pos.reshape(1)])

    def later_loads(start):
        return [
            (0, 0, 0, 0, part),
            (1, start, 1, 0, part),
            (2, 0, 2, 0, part),
            (3, start, 3, 0, part),
            (4, 0, 4, 0, full),
            (5, 0, 5, 0, part),
            (6, 0, 5, part, part),
            (7, 0, 6, 0, part),
            (8, 0, 6, part, part),
        ]

    rights = (p_own, *partner, *beyond)
    earlier = run_products(
        mid_kernel,
        later_codes,
        (a_far[0], p_far, a_last[0], p_last, *rights, partial, kept_1, kept_2),
        later_loads(0)
        + [
            (9, 0, 7, 0, width),
            (10, 0, 8, 0, full),
            (11, 0, 9, 0, full),
        ],
        [piece] * 4 + [whole] * 3 + [square, whole, whole],
        wide,
        band,
        row_count,
        flops,
    )
    keep, send = run_products(
        late_kernel,
        later_codes,
        (a_far[1], p_far, a_last[1], p_last, *rights, earlier),
        later_loads(part) + [(9, 0, 7, 0, width)],
        [piece] * 4 + [whole] * 3 + [wide],
        (half, half),
        band,
        row_count,
        flops,
    )
    share = width // groups
    pair = keep + xor_permute(send, "grp", 1)
    total = pair[:share] + xor_permute(pair[share:], "grp", 2)
    total = total.astype(jnp.bfloat16)
    own, direct, diagonal = (total[:, i * width : (i + 1) * width] for i in range(SLOTS))
    even = rows_pos % 2 == 0
    return jnp.concatenate(
        [jnp.where(even, diagonal, direct), own, jnp.where(even, direct, diagonal)], axis=1
    )


def pack_kernel(names, capacity, pieces, slot_ref, a_hbm, *refs):
    count = len(names)
    outs, (a_ref, packed, sems_in, sems_out) = refs[:count], refs[count:]
    columns = a_ref.shape[1] // pieces
    loads = [
        pltpu.make_async_copy(
            a_hbm.at[:, pl.ds(i * columns, columns)],
            a_ref.at[:, pl.ds(i * columns, columns)],
            sems_in.at[i],
        )
        for i in range(pieces)
    ]
    for copy in loads:
        copy.start()
    shape = (capacity, a_ref.shape[0])
    hot = jnp.concatenate(
        [
            (lax.broadcasted_iota(jnp.int32, shape, 0) + name * capacity == slot_ref[...]).astype(
                jnp.float32
            )
            for name in names
        ],
        axis=0,
    )
    empty = jnp.sum(hot, axis=1, keepdims=True) < 0.5
    hot = hot.astype(jnp.bfloat16)
    stores = []
    for i in range(pieces):
        loads[i].wait()
        at = slice(i * columns, (i + 1) * columns)
        packed[:, at] = jnp.dot(
            hot, a_ref[:, at], preferred_element_type=jnp.float32
        ).astype(jnp.bfloat16)
        if i == 0:
            first = packed[:, :128].astype(jnp.float32)
            packed[:, :128] = jnp.where(empty, jnp.inf, first).astype(jnp.bfloat16)
        for chunk in range(count):
            copy = pltpu.make_async_copy(
                packed.at[pl.ds(chunk * capacity, capacity), pl.ds(i * columns, columns)],
                outs[chunk].at[:, pl.ds(i * columns, columns)],
                sems_out.at[chunk * pieces + i],
            )
            copy.start()
            stores.append(copy)
    for copy in stores:
        copy.wait()


def pack_chunks(a_vals, slot_of, names, capacity):
    row_count, row_width = a_vals.shape
    pieces, count = 4, len(names)
    out = pl.pallas_call(
        functools.partial(pack_kernel, names, capacity, pieces),
        out_shape=[jax.ShapeDtypeStruct((capacity, row_width), a_vals.dtype)] * count,
        in_specs=[pl.BlockSpec(memory_space=pltpu.VMEM), pl.BlockSpec(memory_space=pl.ANY)],
        out_specs=[pl.BlockSpec(memory_space=pl.ANY)] * count,
        scratch_shapes=[
            pltpu.VMEM((row_count, row_width), a_vals.dtype),
            pltpu.VMEM((count * capacity, row_width), a_vals.dtype),
            pltpu.SemaphoreType.DMA((pieces,)),
            pltpu.SemaphoreType.DMA((count * pieces,)),
        ],
    )(slot_of[None, :], a_vals)
    return dict(zip(names, out))


def gather_kernel(names, capacity, where, *refs):
    chunks = len(names)
    sources, (target, probe, buffer, sems_probe, sems_in, sems_out) = refs[:chunks], refs[chunks:]
    me = where[0]
    probes = [
        pltpu.make_async_copy(
            sources[c].at[:, pl.ds(0, probe.shape[2])], probe.at[c], sems_probe.at[c]
        )
        for c in range(chunks)
    ]
    for copy in probes:
        copy.start()
    full = []
    for c in range(chunks):
        probes[c].wait()
        full.append(jnp.where(jnp.max(probe[c].astype(jnp.float32)) < jnp.inf, 1, 0))
    limit = target.shape[0] // capacity - 1
    place = []
    for c in range(chunks):
        sender = jnp.bitwise_xor(me, names[c])
        ahead = jnp.int32(0)
        for other in range(chunks):
            first = jnp.bitwise_xor(me, names[other]) < sender
            ahead = ahead + jnp.where(first, full[other], 0)
        place.append(pl.multiple_of(jnp.minimum(ahead, limit) * capacity, capacity))

    def loads(c):
        return pltpu.make_async_copy(
            sources[c], buffer.at[pl.ds(place[c], capacity), :], sems_in.at[c]
        )

    def stores(c):
        return pltpu.make_async_copy(
            buffer.at[pl.ds(place[c], capacity), :],
            target.at[pl.ds(place[c], capacity), :],
            sems_out.at[c],
        )

    for c in range(chunks):
        pl.when(full[c] == 1)(lambda c=c: loads(c).start())
    for c in range(chunks):
        @pl.when(full[c] == 1)
        def _():
            loads(c).wait()
            stores(c).start()

    for c in range(chunks):
        pl.when(full[c] == 1)(lambda c=c: stores(c).wait())


def gather_chunks(incoming, where, row_count):
    names = tuple(incoming)
    chunks = len(names)
    capacity, row_width = incoming[0].shape
    dtype = incoming[0].dtype
    return pl.pallas_call(
        functools.partial(gather_kernel, names, capacity),
        out_shape=jax.ShapeDtypeStruct((row_count, row_width), dtype),
        in_specs=[pl.BlockSpec(memory_space=pltpu.SMEM)]
        + [pl.BlockSpec(memory_space=pl.ANY)] * chunks,
        out_specs=pl.BlockSpec(memory_space=pl.ANY),
        scratch_shapes=[
            pltpu.VMEM((chunks, capacity, 128), dtype),
            pltpu.VMEM((row_count, row_width), dtype),
            pltpu.SemaphoreType.DMA((chunks,)),
            pltpu.SemaphoreType.DMA((chunks,)),
            pltpu.SemaphoreType.DMA((chunks,)),
        ],
        name="gather_chunks",
    )(where, *incoming.values())


def use_chunks(row_count, rows_total):
    capacity = max(2, 2 * row_count // rows_total)
    return capacity % 16 == 0 and rows_total & (rows_total - 1) == 0


def migrate(a_vals, new_rows):
    row_count, row_width = a_vals.shape
    rows_total = lax.axis_size("rows")
    capacity = max(2, 2 * row_count // rows_total)
    slot_total = rows_total * capacity
    earlier = jnp.arange(row_count)[None, :] < jnp.arange(row_count)[:, None]
    same = new_rows[:, None] == new_rows[None, :]
    ranking = jnp.sum((earlier & same).astype(jnp.int32), axis=1)
    if use_chunks(row_count, rows_total):
        rows_pos = lax.axis_index("rows")
        slot_of = jnp.bitwise_xor(new_rows, rows_pos) * capacity + ranking
        first = tuple(range(rows_total // 2, rows_total, 2))
        rest = tuple(i for i in range(rows_total) if i not in first)
        chunks = pack_chunks(a_vals, slot_of, first, capacity)
        chunks |= pack_chunks(a_vals, slot_of, rest, capacity)
        incoming = {
            bit: xor_permute(chunks[bit], "rows", bit) if bit else chunks[0]
            for bit in range(rows_total)
        }
        return gather_chunks(incoming, rows_pos.astype(jnp.int32).reshape(1), row_count)
    slot_of = new_rows * capacity + ranking
    slot_ids = jnp.arange(slot_total, dtype=jnp.int32)
    sender = slot_ids[:, None] == slot_of[None, :]
    picked = jnp.dot(sender.astype(jnp.bfloat16), a_vals, preferred_element_type=jnp.float32)
    filled = jnp.any(sender, axis=1)
    incoming = lax.all_to_all(
        picked.astype(a_vals.dtype).reshape(rows_total, capacity, row_width),
        "rows",
        split_axis=0,
        concat_axis=0,
        tiled=True,
    ).reshape(slot_total, row_width)
    flags = lax.all_to_all(
        filled.astype(jnp.bfloat16).reshape(rows_total, capacity),
        "rows",
        split_axis=0,
        concat_axis=0,
        tiled=True,
    )
    flat_flags = flags.reshape(slot_total).astype(jnp.float32)
    position = jnp.cumsum(flat_flags) - 1.0
    wanted = jnp.arange(row_count, dtype=jnp.float32)
    receiver = (position[None, :] == wanted[:, None]) & (flat_flags[None, :] > 0.0)
    return jnp.dot(
        receiver.astype(jnp.bfloat16), incoming, preferred_element_type=jnp.float32
    ).astype(a_vals.dtype)


def local(a_vals, a_cols, p_vals, new_rows):
    a_moved = migrate(a_vals, new_rows)
    coarse = galerkin(a_vals, a_cols, p_vals)
    return (a_moved, coarse)


def solution(mesh):
    in_specs = (
        P(("rows", "grp")),
        P(("rows", "grp")),
        P(("rows", "grp")),
        P(("rows", "grp")),
    )
    out_specs = (P(("rows", "grp"), None), P(("rows", "grp"), None))
    return jax.shard_map(local, mesh=mesh, in_specs=in_specs, out_specs=out_specs, check_vma=False)
```

```python
import functools

import jax
import jax.numpy as jnp
from jax import lax
from jax.experimental import pallas as pl
from jax.experimental.pallas import tpu as pltpu
from jax.sharding import PartitionSpec as P


B = 64
UNROLL = 8
SLOTS = 3


def xor_permute(value, axis, bit):
    count = lax.axis_size(axis)
    return lax.ppermute(value, axis, [(i, i ^ bit) for i in range(count)])


def entry_codes(cols, rows_pos, grp_pos, groups):
    row_count, band = cols.shape
    device = cols // row_count
    near = device // groups - rows_pos
    side = jnp.where(rows_pos % 2 == 1, -near, near)
    slot = jnp.where(near == 0, 0, jnp.where(side == 1, 1, 2))
    target = slot * row_count + cols % row_count
    entry = jnp.arange(row_count, dtype=jnp.int32)[:, None] * band + jnp.arange(
        band, dtype=jnp.int32
    )
    code = entry * target_span(row_count) + target
    return jnp.where(device % groups == grp_pos, code, -1).reshape(-1)


def target_span(row_count):
    return pl.next_power_of_2(SLOTS * row_count + 1)


def clear(sums):
    rows = 2 * B

    def step(i, _):
        sums[pl.ds(pl.multiple_of(i * rows, rows), rows), :] = jnp.zeros(
            (rows, sums.shape[1]), sums.dtype
        )
        return 0

    lax.fori_loop(0, sums.shape[0] // rows, step, 0)


def scatter_part(band, row_count, offset, base, code_ref, a_ref, p_ref, sums, order):
    entries = a_ref.shape[0] // B * band
    span = target_span(row_count)
    dummy = base * band * span + SLOTS * row_count

    def collect(step, found):
        code = code_ref[offset + base * band + step]
        order[found] = code
        return found + jnp.where(code >= 0, 1, 0)

    count = lax.fori_loop(0, entries, collect, 0, unroll=16)
    for pad in range(UNROLL):
        order[count + pad] = dummy

    def batch(step, _):
        terms = []
        for lane in range(UNROLL):
            code = order[step * UNROLL + lane]
            target = jnp.bitwise_and(code, span - 1)
            entry = lax.div(code, span)
            row = lax.div(entry, band) - base
            k = lax.rem(entry, band)
            start = pl.multiple_of(row * B, B)
            half = pl.multiple_of(lax.div(k, 2) * (2 * B), 2 * B)
            block = a_ref[pl.ds(start, B), pl.ds(half, 2 * B)]
            block = jnp.where(lax.rem(k, 2) == 1, block[:, B:], block[:, :B])
            left = p_ref[pl.ds(start, B), :]
            terms.append((contract(block, left), target))
        for term, target in terms:
            at = pl.ds(pl.multiple_of(target * B, B), B)
            sums[at, :] = sums[at, :] + term
        return 0

    lax.fori_loop(0, lax.div(count + UNROLL - 1, UNROLL), batch, 0)


def contract(left, right):
    return lax.dot_general(
        left, right, (((0,), (0,)), ((), ())), preferred_element_type=jnp.float32
    )


def copies_of(loads, sources, buffers, sems):
    copies = []
    for i, (source, start, buffer, at, rows) in enumerate(loads):
        copy = pltpu.make_async_copy(
            sources[source].at[pl.ds(start, rows), :],
            buffers[buffer].at[pl.ds(at, rows), :],
            sems.at[i],
        )
        copies.append(copy)
        copy.start()
    return lambda i: copies[i].wait()


def early_kernel(band, row_count, loads, inputs, codes, *refs):
    sources, (partial, kept_1, kept_2), refs = refs[:inputs], refs[inputs : inputs + 3], refs[inputs + 3 :]
    buffers, (sums, order, sems) = refs[:-3], refs[-3:]
    wait = copies_of(loads, sources, buffers, sems)
    clear(sums)
    for part in range(2):
        for i in range(3):
            wait(3 * part + i)
        a_ref, p_ref = buffers[2 * part : 2 * part + 2]
        scatter_part(
            band, row_count, part * row_count * band, 0, codes, a_ref, p_ref, sums, order
        )
    size = row_count * B
    stores = []
    for slot, kept in ((1, kept_1), (2, kept_2)):
        staged = buffers[2 * (slot - 1)]
        staged[...] = sums[slot * size : (slot + 1) * size].astype(jnp.bfloat16)
        stores.append(pltpu.make_async_copy(staged, kept, sems.at[len(loads) + slot - 1]))
        stores[-1].start()
    partial[...] = contract(sums[:size].astype(jnp.bfloat16), buffers[1][...])
    for copy in stores:
        copy.wait()


def later_sums(band, row_count, base, wait, codes, buffers, sums, order):
    clear(sums)
    for part in range(2):
        wait(2 * part)
        wait(2 * part + 1)
        a_ref, p_ref = buffers[2 * part : 2 * part + 2]
        scatter_part(
            band, row_count, part * row_count * band, base, codes, a_ref, p_ref, sums, order
        )


def mid_kernel(band, row_count, loads, inputs, codes, *refs):
    sources, result, refs = refs[:inputs], refs[inputs], refs[inputs + 1 :]
    buffers, (sums, order, sems) = refs[:-3], refs[-3:]
    wait = copies_of(loads, sources, buffers, sems)
    later_sums(band, row_count, 0, wait, codes, buffers, sums, order)
    for i in range(4, len(loads)):
        wait(i)
    size = row_count * B
    rights, partial, kept = buffers[4 : 4 + SLOTS], buffers[4 + SLOTS], buffers[5 + SLOTS :]
    width = partial.shape[1]
    for slot in range(SLOTS):
        right = rights[slot][...]
        here = contract(sums[slot * size : (slot + 1) * size].astype(jnp.bfloat16), right)
        if slot == 0:
            here = here + partial[...]
        else:
            here = here + contract(kept[slot - 1][...], right)
        result[:, slot * width : (slot + 1) * width] = here


def late_kernel(band, row_count, loads, inputs, codes, *refs):
    sources, (keep, send), refs = refs[:inputs], refs[inputs : inputs + 2], refs[inputs + 2 :]
    buffers, (sums, order, sems) = refs[:-3], refs[-3:]
    grp_pos = codes[2 * row_count * band]
    wait = copies_of(loads, sources, buffers, sems)
    later_sums(band, row_count, row_count // 2, wait, codes, buffers, sums, order)
    for i in range(4, len(loads)):
        wait(i)
    size = row_count * B
    rights, earlier = buffers[4 : 4 + SLOTS], buffers[4 + SLOTS]
    width = rights[0].shape[1]
    share = keep.shape[0] // 2
    for slot in range(SLOTS):
        columns = slice(slot * width, (slot + 1) * width)
        here = contract(
            sums[slot * size : (slot + 1) * size].astype(jnp.bfloat16), rights[slot][...]
        )
        here = here + earlier[:, columns]
        for block in range(width // share):
            piece = here[block * share : (block + 1) * share]
            place = jnp.bitwise_xor(block, grp_pos)
            at = pl.ds(pl.multiple_of(lax.div(place, 2) * share, share), share)

            @pl.when(lax.rem(place, 2) == 0)
            def _():
                keep[at, columns] = piece

            @pl.when(lax.rem(place, 2) == 1)
            def _():
                send[at, columns] = piece


def run_products(body, codes, arrays, loads, buffers, outs, band, row_count, flops, out_specs=None):
    width = arrays[0].shape[1]
    return pl.pallas_call(
        functools.partial(body, band, row_count, loads, len(arrays)),
        out_shape=outs,
        in_specs=[pl.BlockSpec(memory_space=pltpu.SMEM)]
        + [pl.BlockSpec(memory_space=pltpu.HBM)] * len(arrays),
        out_specs=out_specs
        or jax.tree.map(lambda _: pl.BlockSpec(memory_space=pltpu.VMEM), outs),
        scratch_shapes=[pltpu.VMEM(x.shape, x.dtype) for x in buffers]
        + [
            pltpu.VMEM(((SLOTS * row_count + 2) * B, width), jnp.float32),
            pltpu.SMEM((row_count * band + UNROLL,), jnp.int32),
            pltpu.SemaphoreType.DMA((len(loads) + 2,)),
        ],
        compiler_params=pltpu.CompilerParams(vmem_limit_bytes=60 << 20),
        cost_estimate=pl.CostEstimate(
            flops=flops,
            bytes_accessed=sum(x.size * x.dtype.itemsize for x in arrays),
            transcendentals=0,
        ),
    )(codes, *arrays)


def galerkin(a_vals, a_cols, p_vals):
    row_count, band = a_cols.shape
    width = p_vals.shape[1] // B
    rows_total, groups = lax.axis_size("rows"), lax.axis_size("grp")
    rows_pos, grp_pos = lax.axis_index("rows"), lax.axis_index("grp")
    assert groups == 4 and rows_total % 2 == 0
    p_own = p_vals.reshape(row_count * B, width)
    cut = row_count // 2
    a_own = [a_vals[i * cut : (i + 1) * cut].reshape(cut * B, band * B) for i in range(2)]

    cut = row_count // 2
    p_own = lax.optimization_barrier(p_own)
    p_half = [p_own[i * cut * B : (i + 1) * cut * B] for i in range(2)]
    partner = [xor_permute(p_half[i], "rows", 1) for i in range(2)]
    onward = [(i, j) for i in range(rows_total) for j in [i - 2 if i % 2 else i + 2]]
    ahead = [(i, j) for i in range(rows_total) for j in [i + 2 if i % 2 else i - 2]]
    onward, ahead = ([p for p in pairs if 0 <= p[1] < rows_total] for pairs in (onward, ahead))
    moved = lax.ppermute(p_half[1], "rows", ahead)
    beyond = [lax.ppermute(partner[0], "rows", onward), xor_permute(moved, "rows", 1)]

    c_far = xor_permute(a_cols, "grp", 2)
    c_near = xor_permute(a_cols, "grp", 1)
    c_last = xor_permute(c_far, "grp", 1)
    p_far = xor_permute(p_own, "grp", 2)
    p_near = xor_permute(p_own, "grp", 1)
    p_last = xor_permute(p_far, "grp", 1)
    a_far = [xor_permute(a_own[i], "grp", 2) for i in range(2)]
    a_near = [xor_permute(a_own[i], "grp", 1) for i in range(2)]
    a_last = [xor_permute(a_far[i], "grp", 1) for i in range(2)]

    def codes(*cols):
        return [entry_codes(c, rows_pos, grp_pos, groups) for c in cols]

    flops = 4 * row_count * band * B * B * width // 2
    full, part = row_count * B, cut * B
    whole = jax.ShapeDtypeStruct((full, width), jnp.bfloat16)
    piece = jax.ShapeDtypeStruct((part, width), jnp.bfloat16)
    square = jax.ShapeDtypeStruct((width, width), jnp.float32)
    wide = jax.ShapeDtypeStruct((width, SLOTS * width), jnp.float32)
    half = jax.ShapeDtypeStruct((width // 2, SLOTS * width), jnp.float32)
    partial, kept_1, kept_2 = run_products(
        early_kernel,
        jnp.concatenate(codes(a_cols, c_near)),
        (*a_own, p_own, *a_near, p_near),
        [
            (0, 0, 0, 0, part),
            (1, 0, 0, part, part),
            (2, 0, 1, 0, full),
            (3, 0, 2, 0, part),
            (4, 0, 2, part, part),
            (5, 0, 3, 0, full),
        ],
        [whole] * 4,
        (square, whole, whole),
        band,
        row_count,
        flops,
        (pl.BlockSpec(memory_space=pltpu.VMEM),) + (pl.BlockSpec(memory_space=pltpu.HBM),) * 2,
    )
    later_codes = jnp.concatenate([*codes(c_far, c_last), grp_pos.reshape(1)])

    def later_loads(start):
        return [
            (0, 0, 0, 0, part),
            (1, start, 1, 0, part),
            (2, 0, 2, 0, part),
            (3, start, 3, 0, part),
            (4, 0, 4, 0, full),
            (5, 0, 5, 0, part),
            (6, 0, 5, part, part),
            (7, 0, 6, 0, part),
            (8, 0, 6, part, part),
        ]

    rights = (p_own, *partner, *beyond)
    earlier = run_products(
        mid_kernel,
        later_codes,
        (a_far[0], p_far, a_last[0], p_last, *rights, partial, kept_1, kept_2),
        later_loads(0)
        + [
            (9, 0, 7, 0, width),
            (10, 0, 8, 0, full),
            (11, 0, 9, 0, full),
        ],
        [piece] * 4 + [whole] * 3 + [square, whole, whole],
        wide,
        band,
        row_count,
        flops,
    )
    keep, send = run_products(
        late_kernel,
        later_codes,
        (a_far[1], p_far, a_last[1], p_last, *rights, earlier),
        later_loads(part) + [(9, 0, 7, 0, width)],
        [piece] * 4 + [whole] * 3 + [wide],
        (half, half),
        band,
        row_count,
        flops,
    )
    share = width // groups
    pair = keep + xor_permute(send, "grp", 1)
    total = pair[:share] + xor_permute(pair[share:], "grp", 2)
    total = total.astype(jnp.bfloat16)
    own, direct, diagonal = (total[:, i * width : (i + 1) * width] for i in range(SLOTS))
    even = rows_pos % 2 == 0
    return jnp.concatenate(
        [jnp.where(even, diagonal, direct), own, jnp.where(even, direct, diagonal)], axis=1
    )


def pack_kernel(names, capacity, pieces, slot_ref, a_hbm, *refs):
    count = len(names)
    outs, (a_ref, packed, sems_in, sems_out) = refs[:count], refs[count:]
    columns = a_ref.shape[1] // pieces
    loads = [
        pltpu.make_async_copy(
            a_hbm.at[:, pl.ds(i * columns, columns)],
            a_ref.at[:, pl.ds(i * columns, columns)],
            sems_in.at[i],
        )
        for i in range(pieces)
    ]
    for copy in loads:
        copy.start()
    shape = (capacity, a_ref.shape[0])
    hot = jnp.concatenate(
        [
            (lax.broadcasted_iota(jnp.int32, shape, 0) + name * capacity == slot_ref[...]).astype(
                jnp.float32
            )
            for name in names
        ],
        axis=0,
    )
    empty = jnp.sum(hot, axis=1, keepdims=True) < 0.5
    hot = hot.astype(jnp.bfloat16)
    stores = []
    for i in range(pieces):
        loads[i].wait()
        at = slice(i * columns, (i + 1) * columns)
        packed[:, at] = jnp.dot(
            hot, a_ref[:, at], preferred_element_type=jnp.float32
        ).astype(jnp.bfloat16)
        if i == 0:
            first = packed[:, :128].astype(jnp.float32)
            packed[:, :128] = jnp.where(empty, jnp.inf, first).astype(jnp.bfloat16)
        for chunk in range(count):
            copy = pltpu.make_async_copy(
                packed.at[pl.ds(chunk * capacity, capacity), pl.ds(i * columns, columns)],
                outs[chunk].at[:, pl.ds(i * columns, columns)],
                sems_out.at[chunk * pieces + i],
            )
            copy.start()
            stores.append(copy)
    for copy in stores:
        copy.wait()


def pack_chunks(a_vals, slot_of, names, capacity):
    row_count, row_width = a_vals.shape
    pieces, count = 4, len(names)
    out = pl.pallas_call(
        functools.partial(pack_kernel, names, capacity, pieces),
        out_shape=[jax.ShapeDtypeStruct((capacity, row_width), a_vals.dtype)] * count,
        in_specs=[pl.BlockSpec(memory_space=pltpu.VMEM), pl.BlockSpec(memory_space=pl.ANY)],
        out_specs=[pl.BlockSpec(memory_space=pl.ANY)] * count,
        scratch_shapes=[
            pltpu.VMEM((row_count, row_width), a_vals.dtype),
            pltpu.VMEM((count * capacity, row_width), a_vals.dtype),
            pltpu.SemaphoreType.DMA((pieces,)),
            pltpu.SemaphoreType.DMA((count * pieces,)),
        ],
    )(slot_of[None, :], a_vals)
    return dict(zip(names, out))


def gather_kernel(names, capacity, where, *refs):
    chunks = len(names)
    sources, (target, buffer, sems_in, sems_out) = refs[:chunks], refs[chunks:]
    me = where[0]
    loads = [
        pltpu.make_async_copy(sources[c], buffer.at[c], sems_in.at[c]) for c in range(chunks)
    ]
    for copy in loads:
        copy.start()
    full = []
    for c in range(chunks):
        loads[c].wait()
        head = buffer[c, :, :128].astype(jnp.float32)
        full.append(jnp.where(jnp.max(head) < jnp.inf, 1, 0))
    limit = target.shape[0] // capacity - 1
    stores = []
    for c in range(chunks):
        sender = jnp.bitwise_xor(me, names[c])
        ahead = jnp.int32(0)
        for other in range(chunks):
            first = jnp.bitwise_xor(me, names[other]) < sender
            ahead = ahead + jnp.where(first, full[other], 0)
        place = pl.multiple_of(jnp.minimum(ahead, limit) * capacity, capacity)
        copy = pltpu.make_async_copy(
            buffer.at[c], target.at[pl.ds(place, capacity), :], sems_out.at[c]
        )
        stores.append(copy)
        pl.when(full[c] == 1)(copy.start)
    for c in range(chunks):
        pl.when(full[c] == 1)(stores[c].wait)


def gather_chunks(incoming, where, row_count):
    names = tuple(incoming)
    chunks = len(names)
    capacity, row_width = incoming[0].shape
    dtype = incoming[0].dtype
    return pl.pallas_call(
        functools.partial(gather_kernel, names, capacity),
        out_shape=jax.ShapeDtypeStruct((row_count, row_width), dtype),
        in_specs=[pl.BlockSpec(memory_space=pltpu.SMEM)]
        + [pl.BlockSpec(memory_space=pl.ANY)] * chunks,
        out_specs=pl.BlockSpec(memory_space=pl.ANY),
        scratch_shapes=[
            pltpu.VMEM((chunks, capacity, row_width), dtype),
            pltpu.SemaphoreType.DMA((chunks,)),
            pltpu.SemaphoreType.DMA((chunks,)),
        ],
        name="gather_chunks",
    )(where, *incoming.values())


def use_chunks(row_count, rows_total):
    capacity = max(2, 2 * row_count // rows_total)
    return capacity % 16 == 0 and rows_total & (rows_total - 1) == 0


def migrate(a_vals, new_rows):
    row_count, row_width = a_vals.shape
    rows_total = lax.axis_size("rows")
    capacity = max(2, 2 * row_count // rows_total)
    slot_total = rows_total * capacity
    earlier = jnp.arange(row_count)[None, :] < jnp.arange(row_count)[:, None]
    same = new_rows[:, None] == new_rows[None, :]
    ranking = jnp.sum((earlier & same).astype(jnp.int32), axis=1)
    if use_chunks(row_count, rows_total):
        rows_pos = lax.axis_index("rows")
        slot_of = jnp.bitwise_xor(new_rows, rows_pos) * capacity + ranking
        first = (rows_total // 2,)
        rest = tuple(i for i in range(rows_total) if i not in first)
        chunks = pack_chunks(a_vals, slot_of, first, capacity)
        chunks |= pack_chunks(a_vals, slot_of, rest, capacity)
        incoming = {
            bit: xor_permute(chunks[bit], "rows", bit) if bit else chunks[0]
            for bit in range(rows_total)
        }
        return gather_chunks(incoming, rows_pos.astype(jnp.int32).reshape(1), row_count)
    slot_of = new_rows * capacity + ranking
    slot_ids = jnp.arange(slot_total, dtype=jnp.int32)
    sender = slot_ids[:, None] == slot_of[None, :]
    picked = jnp.dot(sender.astype(jnp.bfloat16), a_vals, preferred_element_type=jnp.float32)
    filled = jnp.any(sender, axis=1)
    incoming = lax.all_to_all(
        picked.astype(a_vals.dtype).reshape(rows_total, capacity, row_width),
        "rows",
        split_axis=0,
        concat_axis=0,
        tiled=True,
    ).reshape(slot_total, row_width)
    flags = lax.all_to_all(
        filled.astype(jnp.bfloat16).reshape(rows_total, capacity),
        "rows",
        split_axis=0,
        concat_axis=0,
        tiled=True,
    )
    flat_flags = flags.reshape(slot_total).astype(jnp.float32)
    position = jnp.cumsum(flat_flags) - 1.0
    wanted = jnp.arange(row_count, dtype=jnp.float32)
    receiver = (position[None, :] == wanted[:, None]) & (flat_flags[None, :] > 0.0)
    return jnp.dot(
        receiver.astype(jnp.bfloat16), incoming, preferred_element_type=jnp.float32
    ).astype(a_vals.dtype)


def local(a_vals, a_cols, p_vals, new_rows):
    a_moved = migrate(a_vals, new_rows)
    coarse = galerkin(a_vals, a_cols, p_vals)
    return (a_moved, coarse)


def solution(mesh):
    in_specs = (
        P(("rows", "grp")),
        P(("rows", "grp")),
        P(("rows", "grp")),
        P(("rows", "grp")),
    )
    out_specs = (P(("rows", "grp"), None), P(("rows", "grp"), None))
    return jax.shard_map(local, mesh=mesh, in_specs=in_specs, out_specs=out_specs, check_vma=False)
```

```python
import functools

import jax
import jax.numpy as jnp
from jax import lax
from jax.experimental import pallas as pl
from jax.experimental.pallas import tpu as pltpu
from jax.sharding import PartitionSpec as P


B = 64
UNROLL = 8
SLOTS = 3


def xor_permute(value, axis, bit):
    count = lax.axis_size(axis)
    return lax.ppermute(value, axis, [(i, i ^ bit) for i in range(count)])


def entry_codes(cols, rows_pos, grp_pos, groups):
    row_count, band = cols.shape
    device = cols // row_count
    near = device // groups - rows_pos
    side = jnp.where(rows_pos % 2 == 1, -near, near)
    slot = jnp.where(near == 0, 0, jnp.where(side == 1, 1, 2))
    target = slot * row_count + cols % row_count
    entry = jnp.arange(row_count, dtype=jnp.int32)[:, None] * band + jnp.arange(
        band, dtype=jnp.int32
    )
    code = entry * target_span(row_count) + target
    return jnp.where(device % groups == grp_pos, code, -1).reshape(-1)


def target_span(row_count):
    return pl.next_power_of_2(SLOTS * row_count + 1)


def clear(sums):
    rows = 2 * B

    def step(i, _):
        sums[pl.ds(pl.multiple_of(i * rows, rows), rows), :] = jnp.zeros(
            (rows, sums.shape[1]), sums.dtype
        )
        return 0

    lax.fori_loop(0, sums.shape[0] // rows, step, 0)


def scatter_part(band, row_count, offset, base, code_ref, a_ref, p_ref, sums, order):
    entries = a_ref.shape[0] // B * band
    span = target_span(row_count)
    dummy = base * band * span + SLOTS * row_count

    def collect(step, found):
        code = code_ref[offset + base * band + step]
        order[found] = code
        return found + jnp.where(code >= 0, 1, 0)

    count = lax.fori_loop(0, entries, collect, 0, unroll=16)
    for pad in range(UNROLL):
        order[count + pad] = dummy

    def batch(step, _):
        terms = []
        for lane in range(UNROLL):
            code = order[step * UNROLL + lane]
            target = jnp.bitwise_and(code, span - 1)
            entry = lax.div(code, span)
            row = lax.div(entry, band) - base
            k = lax.rem(entry, band)
            start = pl.multiple_of(row * B, B)
            half = pl.multiple_of(lax.div(k, 2) * (2 * B), 2 * B)
            block = a_ref[pl.ds(start, B), pl.ds(half, 2 * B)]
            block = jnp.where(lax.rem(k, 2) == 1, block[:, B:], block[:, :B])
            left = p_ref[pl.ds(start, B), :]
            terms.append((contract(block, left), target))
        for term, target in terms:
            at = pl.ds(pl.multiple_of(target * B, B), B)
            sums[at, :] = sums[at, :] + term
        return 0

    lax.fori_loop(0, lax.div(count + UNROLL - 1, UNROLL), batch, 0)


def contract(left, right):
    return lax.dot_general(
        left, right, (((0,), (0,)), ((), ())), preferred_element_type=jnp.float32
    )


def copies_of(loads, sources, buffers, sems):
    copies = []
    for i, (source, start, buffer, at, rows) in enumerate(loads):
        copy = pltpu.make_async_copy(
            sources[source].at[pl.ds(start, rows), :],
            buffers[buffer].at[pl.ds(at, rows), :],
            sems.at[i],
        )
        copies.append(copy)
        copy.start()
    return lambda i: copies[i].wait()


def early_kernel(band, row_count, loads, inputs, codes, *refs):
    sources, (partial, kept_1, kept_2), refs = refs[:inputs], refs[inputs : inputs + 3], refs[inputs + 3 :]
    buffers, (sums, order, sems) = refs[:-3], refs[-3:]
    wait = copies_of(loads, sources, buffers, sems)
    clear(sums)
    for part in range(2):
        for i in range(3):
            wait(3 * part + i)
        a_ref, p_ref = buffers[2 * part : 2 * part + 2]
        scatter_part(
            band, row_count, part * row_count * band, 0, codes, a_ref, p_ref, sums, order
        )
    size = row_count * B
    stores = []
    for slot, kept in ((1, kept_1), (2, kept_2)):
        staged = buffers[2 * (slot - 1)]
        staged[...] = sums[slot * size : (slot + 1) * size].astype(jnp.bfloat16)
        stores.append(pltpu.make_async_copy(staged, kept, sems.at[len(loads) + slot - 1]))
        stores[-1].start()
    partial[...] = contract(sums[:size].astype(jnp.bfloat16), buffers[1][...])
    for copy in stores:
        copy.wait()


def later_sums(band, row_count, base, wait, codes, buffers, sums, order):
    clear(sums)
    for part in range(2):
        wait(2 * part)
        wait(2 * part + 1)
        a_ref, p_ref = buffers[2 * part : 2 * part + 2]
        scatter_part(
            band, row_count, part * row_count * band, base, codes, a_ref, p_ref, sums, order
        )


def mid_kernel(band, row_count, loads, inputs, codes, *refs):
    sources, result, refs = refs[:inputs], refs[inputs], refs[inputs + 1 :]
    buffers, (sums, order, sems) = refs[:-3], refs[-3:]
    wait = copies_of(loads, sources, buffers, sems)
    later_sums(band, row_count, 0, wait, codes, buffers, sums, order)
    for i in range(4, len(loads)):
        wait(i)
    size = row_count * B
    rights, partial, kept = buffers[4 : 4 + SLOTS], buffers[4 + SLOTS], buffers[5 + SLOTS :]
    width = partial.shape[1]
    for slot in range(SLOTS):
        right = rights[slot][...]
        here = contract(sums[slot * size : (slot + 1) * size].astype(jnp.bfloat16), right)
        if slot == 0:
            here = here + partial[...]
        else:
            here = here + contract(kept[slot - 1][...], right)
        result[:, slot * width : (slot + 1) * width] = here


def late_kernel(band, row_count, loads, inputs, codes, *refs):
    sources, (keep, send), refs = refs[:inputs], refs[inputs : inputs + 2], refs[inputs + 2 :]
    buffers, (sums, order, sems) = refs[:-3], refs[-3:]
    grp_pos = codes[2 * row_count * band]
    wait = copies_of(loads, sources, buffers, sems)
    later_sums(band, row_count, row_count // 2, wait, codes, buffers, sums, order)
    for i in range(4, len(loads)):
        wait(i)
    size = row_count * B
    rights, earlier = buffers[4 : 4 + SLOTS], buffers[4 + SLOTS]
    width = rights[0].shape[1]
    share = keep.shape[0] // 2
    for slot in range(SLOTS):
        columns = slice(slot * width, (slot + 1) * width)
        here = contract(
            sums[slot * size : (slot + 1) * size].astype(jnp.bfloat16), rights[slot][...]
        )
        here = here + earlier[:, columns]
        for block in range(width // share):
            piece = here[block * share : (block + 1) * share]
            place = jnp.bitwise_xor(block, grp_pos)
            at = pl.ds(pl.multiple_of(lax.div(place, 2) * share, share), share)

            @pl.when(lax.rem(place, 2) == 0)
            def _():
                keep[at, columns] = piece

            @pl.when(lax.rem(place, 2) == 1)
            def _():
                send[at, columns] = piece


def run_products(body, codes, arrays, loads, buffers, outs, band, row_count, flops, out_specs=None):
    width = arrays[0].shape[1]
    held = sum(x.size * x.dtype.itemsize for x in buffers) + SLOTS * row_count * B * width * 4
    return pl.pallas_call(
        functools.partial(body, band, row_count, loads, len(arrays)),
        out_shape=outs,
        in_specs=[pl.BlockSpec(memory_space=pltpu.SMEM)]
        + [pl.BlockSpec(memory_space=pl.ANY)] * len(arrays),
        out_specs=out_specs
        or jax.tree.map(lambda _: pl.BlockSpec(memory_space=pltpu.VMEM), outs),
        scratch_shapes=[pltpu.VMEM(x.shape, x.dtype) for x in buffers]
        + [
            pltpu.VMEM(((SLOTS * row_count + 2) * B, width), jnp.float32),
            pltpu.SMEM((row_count * band + UNROLL,), jnp.int32),
            pltpu.SemaphoreType.DMA((len(loads) + 2,)),
        ],
        compiler_params=pltpu.CompilerParams(vmem_limit_bytes=held + (16 << 20)),
        cost_estimate=pl.CostEstimate(
            flops=flops,
            bytes_accessed=sum(x.size * x.dtype.itemsize for x in arrays),
            transcendentals=0,
        ),
    )(codes, *arrays)


def galerkin(a_vals, a_cols, p_vals):
    row_count, band = a_cols.shape
    width = p_vals.shape[1] // B
    rows_total, groups = lax.axis_size("rows"), lax.axis_size("grp")
    rows_pos, grp_pos = lax.axis_index("rows"), lax.axis_index("grp")
    assert groups == 4 and rows_total % 2 == 0
    p_own = p_vals.reshape(row_count * B, width)
    cut = row_count // 2
    a_own = [a_vals[i * cut : (i + 1) * cut].reshape(cut * B, band * B) for i in range(2)]

    cut = row_count // 2
    p_own = lax.optimization_barrier(p_own)
    p_half = [p_own[i * cut * B : (i + 1) * cut * B] for i in range(2)]
    partner = [xor_permute(p_half[i], "rows", 1) for i in range(2)]
    onward = [(i, j) for i in range(rows_total) for j in [i - 2 if i % 2 else i + 2]]
    ahead = [(i, j) for i in range(rows_total) for j in [i + 2 if i % 2 else i - 2]]
    onward, ahead = ([p for p in pairs if 0 <= p[1] < rows_total] for pairs in (onward, ahead))
    moved = lax.ppermute(p_half[1], "rows", ahead)
    beyond = [lax.ppermute(partner[0], "rows", onward), xor_permute(moved, "rows", 1)]

    c_far = xor_permute(a_cols, "grp", 2)
    c_near = xor_permute(a_cols, "grp", 1)
    c_last = xor_permute(c_far, "grp", 1)
    p_far = xor_permute(p_own, "grp", 2)
    p_near = xor_permute(p_own, "grp", 1)
    p_last = xor_permute(p_far, "grp", 1)
    a_far = [xor_permute(a_own[i], "grp", 2) for i in range(2)]
    a_near = [xor_permute(a_own[i], "grp", 1) for i in range(2)]
    a_last = [xor_permute(a_far[i], "grp", 1) for i in range(2)]

    def codes(*cols):
        return [entry_codes(c, rows_pos, grp_pos, groups) for c in cols]

    flops = 4 * row_count * band * B * B * width // 2
    full, part = row_count * B, cut * B
    whole = jax.ShapeDtypeStruct((full, width), jnp.bfloat16)
    piece = jax.ShapeDtypeStruct((part, width), jnp.bfloat16)
    square = jax.ShapeDtypeStruct((width, width), jnp.float32)
    wide = jax.ShapeDtypeStruct((width, SLOTS * width), jnp.float32)
    half = jax.ShapeDtypeStruct((width // 2, SLOTS * width), jnp.float32)
    partial, kept_1, kept_2 = run_products(
        early_kernel,
        jnp.concatenate(codes(a_cols, c_near)),
        (*a_own, p_own, *a_near, p_near),
        [
            (0, 0, 0, 0, part),
            (1, 0, 0, part, part),
            (2, 0, 1, 0, full),
            (3, 0, 2, 0, part),
            (4, 0, 2, part, part),
            (5, 0, 3, 0, full),
        ],
        [whole] * 4,
        (square, whole, whole),
        band,
        row_count,
        flops,
        (pl.BlockSpec(memory_space=pltpu.VMEM),) + (pl.BlockSpec(memory_space=pltpu.HBM),) * 2,
    )
    later_codes = jnp.concatenate([*codes(c_far, c_last), grp_pos.reshape(1)])

    def later_loads(start):
        return [
            (0, 0, 0, 0, part),
            (1, start, 1, 0, part),
            (2, 0, 2, 0, part),
            (3, start, 3, 0, part),
            (4, 0, 4, 0, full),
            (5, 0, 5, 0, part),
            (6, 0, 5, part, part),
            (7, 0, 6, 0, part),
            (8, 0, 6, part, part),
        ]

    rights = (p_own, *partner, *beyond)
    earlier = run_products(
        mid_kernel,
        later_codes,
        (a_far[0], p_far, a_last[0], p_last, *rights, partial, kept_1, kept_2),
        later_loads(0)
        + [
            (9, 0, 7, 0, width),
            (10, 0, 8, 0, full),
            (11, 0, 9, 0, full),
        ],
        [piece] * 4 + [whole] * 3 + [square, whole, whole],
        wide,
        band,
        row_count,
        flops,
    )
    keep, send = run_products(
        late_kernel,
        later_codes,
        (a_far[1], p_far, a_last[1], p_last, *rights, earlier),
        later_loads(part) + [(9, 0, 7, 0, width)],
        [piece] * 4 + [whole] * 3 + [wide],
        (half, half),
        band,
        row_count,
        flops,
    )
    share = width // groups
    pair = keep + xor_permute(send, "grp", 1)
    total = pair[:share] + xor_permute(pair[share:], "grp", 2)
    total = total.astype(jnp.bfloat16)
    own, direct, diagonal = (total[:, i * width : (i + 1) * width] for i in range(SLOTS))
    even = rows_pos % 2 == 0
    return jnp.concatenate(
        [jnp.where(even, diagonal, direct), own, jnp.where(even, direct, diagonal)], axis=1
    )


def pack_kernel(names, capacity, pieces, slot_ref, a_hbm, *refs):
    count = len(names)
    outs, (a_ref, packed, sems_in, sems_out) = refs[:count], refs[count:]
    columns = a_ref.shape[1] // pieces
    loads = [
        pltpu.make_async_copy(
            a_hbm.at[:, pl.ds(i * columns, columns)],
            a_ref.at[:, pl.ds(i * columns, columns)],
            sems_in.at[i],
        )
        for i in range(pieces)
    ]
    for copy in loads:
        copy.start()
    shape = (capacity, a_ref.shape[0])
    hot = jnp.concatenate(
        [
            (lax.broadcasted_iota(jnp.int32, shape, 0) + name * capacity == slot_ref[...]).astype(
                jnp.float32
            )
            for name in names
        ],
        axis=0,
    )
    empty = jnp.sum(hot, axis=1, keepdims=True) < 0.5
    hot = hot.astype(jnp.bfloat16)
    stores = []
    for i in range(pieces):
        loads[i].wait()
        at = slice(i * columns, (i + 1) * columns)
        packed[:, at] = jnp.dot(
            hot, a_ref[:, at], preferred_element_type=jnp.float32
        ).astype(jnp.bfloat16)
        if i == 0:
            first = packed[:, :128].astype(jnp.float32)
            packed[:, :128] = jnp.where(empty, jnp.inf, first).astype(jnp.bfloat16)
        for chunk in range(count):
            copy = pltpu.make_async_copy(
                packed.at[pl.ds(chunk * capacity, capacity), pl.ds(i * columns, columns)],
                outs[chunk].at[:, pl.ds(i * columns, columns)],
                sems_out.at[chunk * pieces + i],
            )
            copy.start()
            stores.append(copy)
    for copy in stores:
        copy.wait()


def pack_chunks(a_vals, slot_of, names, capacity):
    row_count, row_width = a_vals.shape
    pieces, count = 4, len(names)
    out = pl.pallas_call(
        functools.partial(pack_kernel, names, capacity, pieces),
        out_shape=[jax.ShapeDtypeStruct((capacity, row_width), a_vals.dtype)] * count,
        in_specs=[pl.BlockSpec(memory_space=pltpu.VMEM), pl.BlockSpec(memory_space=pl.ANY)],
        out_specs=[pl.BlockSpec(memory_space=pl.ANY)] * count,
        scratch_shapes=[
            pltpu.VMEM((row_count, row_width), a_vals.dtype),
            pltpu.VMEM((count * capacity, row_width), a_vals.dtype),
            pltpu.SemaphoreType.DMA((pieces,)),
            pltpu.SemaphoreType.DMA((count * pieces,)),
        ],
    )(slot_of[None, :], a_vals)
    return dict(zip(names, out))


def gather_kernel(names, capacity, where, *refs):
    chunks = len(names)
    sources, (target, buffer, sems_in, sems_out) = refs[:chunks], refs[chunks:]
    me = where[0]
    loads = [
        pltpu.make_async_copy(sources[c], buffer.at[c], sems_in.at[c]) for c in range(chunks)
    ]
    for copy in loads:
        copy.start()
    full = []
    for c in range(chunks):
        loads[c].wait()
        head = buffer[c, :, :128].astype(jnp.float32)
        full.append(jnp.where(jnp.max(head) < jnp.inf, 1, 0))
    limit = target.shape[0] // capacity - 1
    stores = []
    for c in range(chunks):
        sender = jnp.bitwise_xor(me, names[c])
        ahead = jnp.int32(0)
        for other in range(chunks):
            first = jnp.bitwise_xor(me, names[other]) < sender
            ahead = ahead + jnp.where(first, full[other], 0)
        place = pl.multiple_of(jnp.minimum(ahead, limit) * capacity, capacity)
        copy = pltpu.make_async_copy(
            buffer.at[c], target.at[pl.ds(place, capacity), :], sems_out.at[c]
        )
        stores.append(copy)
        pl.when(full[c] == 1)(copy.start)
    for c in range(chunks):
        pl.when(full[c] == 1)(stores[c].wait)


def gather_chunks(incoming, where, row_count):
    names = tuple(incoming)
    chunks = len(names)
    capacity, row_width = incoming[0].shape
    dtype = incoming[0].dtype
    return pl.pallas_call(
        functools.partial(gather_kernel, names, capacity),
        out_shape=jax.ShapeDtypeStruct((row_count, row_width), dtype),
        in_specs=[pl.BlockSpec(memory_space=pltpu.SMEM)]
        + [pl.BlockSpec(memory_space=pl.ANY)] * chunks,
        out_specs=pl.BlockSpec(memory_space=pl.ANY),
        scratch_shapes=[
            pltpu.VMEM((chunks, capacity, row_width), dtype),
            pltpu.SemaphoreType.DMA((chunks,)),
            pltpu.SemaphoreType.DMA((chunks,)),
        ],
        name="gather_chunks",
    )(where, *incoming.values())


def use_chunks(row_count, rows_total):
    capacity = max(2, 2 * row_count // rows_total)
    return capacity % 16 == 0 and rows_total & (rows_total - 1) == 0


def migrate(a_vals, new_rows):
    row_count, row_width = a_vals.shape
    rows_total = lax.axis_size("rows")
    capacity = max(2, 2 * row_count // rows_total)
    slot_total = rows_total * capacity
    earlier = jnp.arange(row_count)[None, :] < jnp.arange(row_count)[:, None]
    same = new_rows[:, None] == new_rows[None, :]
    ranking = jnp.sum((earlier & same).astype(jnp.int32), axis=1)
    if use_chunks(row_count, rows_total):
        rows_pos = lax.axis_index("rows")
        slot_of = jnp.bitwise_xor(new_rows, rows_pos) * capacity + ranking
        first = (rows_total // 2,)
        rest = tuple(i for i in range(rows_total) if i not in first)
        chunks = pack_chunks(a_vals, slot_of, first, capacity)
        chunks |= pack_chunks(a_vals, slot_of, rest, capacity)
        incoming = {
            bit: xor_permute(chunks[bit], "rows", bit) if bit else chunks[0]
            for bit in range(rows_total)
        }
        return gather_chunks(incoming, rows_pos.astype(jnp.int32).reshape(1), row_count)
    slot_of = new_rows * capacity + ranking
    slot_ids = jnp.arange(slot_total, dtype=jnp.int32)
    sender = slot_ids[:, None] == slot_of[None, :]
    picked = jnp.dot(sender.astype(jnp.bfloat16), a_vals, preferred_element_type=jnp.float32)
    filled = jnp.any(sender, axis=1)
    incoming = lax.all_to_all(
        picked.astype(a_vals.dtype).reshape(rows_total, capacity, row_width),
        "rows",
        split_axis=0,
        concat_axis=0,
        tiled=True,
    ).reshape(slot_total, row_width)
    flags = lax.all_to_all(
        filled.astype(jnp.bfloat16).reshape(rows_total, capacity),
        "rows",
        split_axis=0,
        concat_axis=0,
        tiled=True,
    )
    flat_flags = flags.reshape(slot_total).astype(jnp.float32)
    position = jnp.cumsum(flat_flags) - 1.0
    wanted = jnp.arange(row_count, dtype=jnp.float32)
    receiver = (position[None, :] == wanted[:, None]) & (flat_flags[None, :] > 0.0)
    return jnp.dot(
        receiver.astype(jnp.bfloat16), incoming, preferred_element_type=jnp.float32
    ).astype(a_vals.dtype)


def local(a_vals, a_cols, p_vals, new_rows):
    a_moved = migrate(a_vals, new_rows)
    coarse = galerkin(a_vals, a_cols, p_vals)
    return (a_moved, coarse)


def solution(mesh):
    in_specs = (
        P(("rows", "grp")),
        P(("rows", "grp")),
        P(("rows", "grp")),
        P(("rows", "grp")),
    )
    out_specs = (P(("rows", "grp"), None), P(("rows", "grp"), None))
    return jax.shard_map(local, mesh=mesh, in_specs=in_specs, out_specs=out_specs, check_vma=False)
```
